1024 devices in a mesh: gx: 32 (over y, z_hi, x), gy: 16 (over z_lo), ta: 2 (over core).
Axes of the slice: x: 4, y: 4, z: 32 (z_hi: 2, z_lo: 16; z = z_hi * 16 + z_lo), core: 2. Of those that a mesh axis runs over, the one named last changes fastest.
Arguments:
- residual: float32 [8192, 64], P(('gx', 'gy', 'ta')), may hold values from -6 to 6
- fine_ops: bfloat16 [8192, 64, 512], P(('gx', 'gy', 'ta')), as said below
- neighbours: int32 [8192, 6], P(('gx', 'gy', 'ta')), may hold values from 0 to 7
- fine_map: int32 [8192], P(('gx', 'gy', 'ta')), may hold values from 0 to 7, as said below
- coarse_maps: int32 [1024, 3, 8], P(('gx', 'gy', 'ta')), may hold values from 0 to 7, as said below
Outputs:
- correction: float32 [8192, 64], P(('gx', 'gy', 'ta'))
The draws below stay inside these ranges and needn't reach their ends.
Inputs may be any that keep to these rules, and one draw needn't show every extreme that they name: `fine_ops`: slot 0 of every block row is its diagonal block, whose diagonal entries are positive. `fine_map`: gives each fine block its coarse block in the level-0 node (the two devices of one ta index whose gx+gy indices differ only in bit 0); over such a pair each value is taken by exactly 2 blocks. `coarse_maps`: row l of a device maps the coarse blocks of its level-l node (the 2 ** (l + 1) devices of one ta index whose gx+gy indices agree above bit l) to those of the level-(l + 1) node; the row is the same on all devices of the level-l node, and over the two level-l nodes of one parent each value is taken exactly twice.
All inputs are finite; a program needn't handle non-finite values.
Results may differ from the reference program's by a relative error of at most 0.0019.
Values may be sent and summed in bfloat16 or wider, within the bound.
No kernel may reach another device: no remote copies, remote signals or barrier semaphores. Data moves between devices by JAX's collectives and lax.ppermute only.
A program may use at most 32 MiB of HBM per device.

```python
import jax
import jax.numpy as jnp
from jax import lax

BLOCK = 64
SLOTS = 8
NEIGHB = 6
COARSE = 8
LEVELS = 4
NEWTON = 4
FINE_BLOCKS = 8
NBLK = 8192
N_TA = 2
DEVICES = 1024


def draw_fine_ops(key, part):
    total_rows = FINE_BLOCKS * DEVICES
    key_noise, key_diag, key_couple = jax.random.split(key, 3)
    full_shape = (total_rows, SLOTS, BLOCK, BLOCK)
    jitter = 0.03 * jax.random.normal(key_noise, full_shape, jnp.float32)
    diag_vals = jax.random.uniform(key_diag, (total_rows, BLOCK), jnp.float32, 0.8, 1.25)
    coupling = jax.random.uniform(key_couple, (total_rows, SLOTS - 1), jnp.float32, 0.06, 0.18)
    identity = jnp.eye(BLOCK, dtype=jnp.float32)
    diagonal_part = identity[None] * diag_vals[:, None, :]
    coupling_part = -coupling[:, :, None, None] * identity
    blocks = jnp.concatenate([diagonal_part[:, None], coupling_part], axis=1) + jitter
    return jnp.transpose(blocks, (0, 2, 1, 3)).reshape(total_rows, BLOCK, SLOTS * BLOCK).astype(jnp.bfloat16)


def split_maps(key, span, width, divisor):
    group_total = DEVICES // N_TA
    device_ids = jnp.arange(DEVICES, dtype=jnp.int32)
    column_pos = device_ids // N_TA
    slab_ids = device_ids % N_TA
    parents = column_pos // (2 * span) * N_TA + slab_ids
    upper_half = column_pos // span % 2
    parent_total = group_total // (2 * span) * N_TA
    perms = jax.vmap(lambda one_key: jax.random.permutation(one_key, 2 * width))(jax.random.split(key, parent_total))
    picked = perms[parents]
    offsets = upper_half[:, None] * width + jnp.arange(width, dtype=jnp.int32)[None]
    chosen = jnp.take_along_axis(picked, offsets, axis=1)
    return (chosen // divisor).astype(jnp.int32)


def draw_fine_map(key, part):
    mapped = split_maps(key, 1, FINE_BLOCKS, 2 * FINE_BLOCKS // COARSE)
    return mapped.reshape(-1).astype(jnp.int32)


def draw_coarse_maps(key, part):
    layers = []
    for section_num in range(LEVELS - 1):
        layers.append(split_maps(jax.random.fold_in(key, section_num + 11), 2 ** (section_num + 1), COARSE, 2))
    return jnp.stack(layers, axis=1).astype(jnp.int32)


def set_ends(array, own_key, low, top_value):
    longest = array.shape.index(max(array.shape))
    spots = []
    for shift in (0, 1):
        where = [jax.random.randint(jax.random.fold_in(own_key, axis), (), 0, length) for axis, length in enumerate(array.shape)]
        where[longest] = (where[longest] + shift) % array.shape[longest]
        spots.append(tuple(where))
    return array.at[spots[0]].set(low).at[spots[1]].set(top_value)


def levels(stream_key, shape, pieces, low, high):
    loudness = 1.0
    for axis_at, shards_of in pieces:
        steps = jax.random.uniform(jax.random.fold_in(jax.random.fold_in(stream_key, 6), axis_at), (shards_of,), jnp.float32, low / len(pieces), high / len(pieces))
        loudness = loudness * jnp.repeat(jnp.exp(steps), shape[axis_at] // shards_of).reshape((-1,) + (1,) * (len(shape) - 1 - axis_at))
    return loudness


def gaussian(rng, extent, deviation, limit, cuts=(), kind=jnp.bfloat16):
    level = levels(rng, extent, cuts, -0.22, 0.18) if cuts else 1.0
    drawn = jax.random.normal(rng, extent, jnp.float32) * deviation * level
    return jnp.minimum(jnp.maximum(drawn, -limit), limit).astype(kind)


def setup_inputs(seed: int = 0) -> dict:
    key_of = jax.random.split(jax.random.key(seed), 6)
    return {
        "residual": gaussian(key_of[0], (NBLK, BLOCK), 1.0, 6.0, ((0, 1024),), jnp.float32),
        "fine_ops": draw_fine_ops(jax.random.fold_in(key_of[5], 71), 0),
        "neighbours": set_ends(jax.random.randint(key_of[2], (NBLK, NEIGHB), 0, FINE_BLOCKS), jax.random.fold_in(key_of[2], 1), 0, FINE_BLOCKS - 1).astype(jnp.int32),
        "fine_map": draw_fine_map(jax.random.fold_in(key_of[5], 71), 0),
        "coarse_maps": draw_coarse_maps(jax.random.fold_in(key_of[5], 71), 0),
    }


exact_mode = lax.Precision.HIGHEST


def newton(blocks):
    width = blocks.shape[-1]
    identity = jnp.eye(width, dtype=blocks.dtype)
    scaling = jnp.mean(jnp.diagonal(blocks, axis1=-2, axis2=-1), axis=-1)
    approx = identity * (1.0 / scaling)[..., None, None]
    for repeat in range(NEWTON):
        product = jnp.matmul(blocks, approx, precision=exact_mode)
        approx = jnp.matmul(approx, 2.0 * identity - product, precision=exact_mode)
    return approx


def one_hot(labels, classes, out_type):
    return (labels[..., None] == jnp.arange(classes, dtype=jnp.int32)).astype(out_type)


def pair_sum(values):
    halves = values.reshape((values.shape[0] // 2, 2) + values.shape[1:])
    return halves[:, 0] + halves[:, 1]


def diag_blocks(coarse_tile):
    shaped = coarse_tile.reshape(coarse_tile.shape[:-2] + (COARSE, BLOCK, COARSE, BLOCK))
    return jnp.moveaxis(jnp.diagonal(shaped, axis1=-4, axis2=-2), -1, -3)


def coarsen(coarse_tile, maps_now):
    select = one_hot(maps_now, COARSE, coarse_tile.dtype)
    shaped = coarse_tile.reshape(coarse_tile.shape[:-2] + (COARSE, BLOCK, COARSE, BLOCK))
    left_side = jnp.einsum('...paqb,...px->...xaqb', shaped, select, precision=exact_mode)
    both_sides = jnp.einsum('...xaqb,...qy->...xayb', left_side, select, precision=exact_mode)
    return both_sides.reshape(coarse_tile.shape)


def restrict_rows(values, maps_now):
    return jnp.einsum('...px,...pa->...xa', one_hot(maps_now, COARSE, values.dtype), values, precision=exact_mode)


def apply_tile(coarse_tile, values):
    flat = values.reshape(values.shape[:-2] + (COARSE * BLOCK,))
    return jnp.einsum('...mn,...n->...m', coarse_tile, flat, precision=exact_mode).reshape(values.shape)


def prolong(coarse_vals, maps_now):
    return jnp.einsum('...px,...xa->...pa', one_hot(maps_now, COARSE, coarse_vals.dtype), coarse_vals, precision=exact_mode)


def reference(residual, fine_ops, neighbours, fine_map, coarse_maps):
    group_total = DEVICES // N_TA
    ops_dev = fine_ops.reshape(DEVICES, FINE_BLOCKS, BLOCK, SLOTS * BLOCK)
    resid_dev = residual.reshape(DEVICES, FINE_BLOCKS, BLOCK)
    cols_dev = neighbours.reshape(DEVICES, FINE_BLOCKS, NEIGHB)
    fmap_dev = fine_map.reshape(DEVICES, FINE_BLOCKS)

    def smooth_fine(packed):
        ops_one, resid_one = packed
        inverse = newton(ops_one[:, :, :BLOCK].astype(jnp.float32))
        return jnp.einsum('nab,nb->na', inverse, resid_one, precision=exact_mode)

    fine_smooth = lax.map(smooth_fine, (ops_dev, resid_dev))
    rounded = fine_smooth.astype(jnp.bfloat16)
    slabs = rounded.reshape(group_total, N_TA, FINE_BLOCKS, BLOCK)
    earlier = jnp.concatenate([jnp.zeros_like(slabs[:, :1]), slabs[:, :-1]], axis=1)
    earlier = earlier.reshape(DEVICES, FINE_BLOCKS, BLOCK)

    def restrict_fine(packed):
        ops_one, resid_one, own_vals, prior_vals, cols_one, map_one = packed
        nearby = own_vals[cols_one]
        stacked = jnp.concatenate([own_vals[:, None], nearby, prior_vals[:, None]], axis=1)
        stacked = stacked.reshape(FINE_BLOCKS, SLOTS * BLOCK)
        applied = jnp.einsum('nam,nm->na', ops_one.astype(jnp.float32), stacked.astype(jnp.float32), precision=exact_mode)
        fine_resid = resid_one - applied
        targets = jnp.concatenate([map_one[:, None], map_one[cols_one]], axis=1)
        select = one_hot(map_one, COARSE, jnp.float32)
        target_hot = one_hot(targets, COARSE, jnp.float32)
        spatial = ops_one[:, :, :(NEIGHB + 1) * BLOCK].reshape(FINE_BLOCKS, BLOCK, NEIGHB + 1, BLOCK).astype(jnp.float32)
        moved = jnp.einsum('nkq,nakb->naqb', target_hot, spatial, precision=exact_mode)
        coarse_tile = jnp.einsum('np,naqb->paqb', select, moved, precision=exact_mode)
        coarse_tile = coarse_tile.reshape(COARSE * BLOCK, COARSE * BLOCK)
        coarse_rows = jnp.einsum('np,na->pa', select, fine_resid, precision=exact_mode)
        return coarse_tile, coarse_rows

    tiles_all, rows_all = lax.map(restrict_fine, (ops_dev, resid_dev, rounded, earlier, cols_dev, fmap_dev))
    tiles_all = tiles_all.reshape(group_total, N_TA, COARSE * BLOCK, COARSE * BLOCK)
    rows_all = rows_all.reshape(group_total, N_TA, COARSE, BLOCK)
    maps_all = coarse_maps.reshape(group_total, N_TA, LEVELS - 1, COARSE)
    level_vals = []
    for section_num in range(LEVELS):
        tiles_all = pair_sum(tiles_all)
        rows_all = pair_sum(rows_all)
        inverse = newton(diag_blocks(tiles_all))
        smoothed = jnp.einsum('...pab,...pb->...pa', inverse, rows_all, precision=exact_mode)
        level_vals.append(smoothed)
        if section_num < LEVELS - 1:
            maps_now = maps_all[:: 2 ** (section_num + 1), :, section_num]
            leftover = rows_all - apply_tile(tiles_all, smoothed)
            tiles_all = coarsen(tiles_all, maps_now)
            rows_all = restrict_rows(leftover, maps_now)
    correction_now = level_vals[-1]
    for section_num in range(LEVELS - 2, -1, -1):
        maps_now = maps_all[:: 2 ** (section_num + 1), :, section_num]
        widened = jnp.repeat(correction_now, 2, axis=0)
        correction_now = level_vals[section_num] + prolong(widened, maps_now)
    per_device = jnp.repeat(correction_now, 2, axis=0).reshape(DEVICES, COARSE, BLOCK)
    fine_part = jnp.einsum('npx,nxa->npa', one_hot(fmap_dev, COARSE, jnp.float32), per_device, precision=exact_mode)
    return (fine_smooth + fine_part).reshape(DEVICES * FINE_BLOCKS, BLOCK)
```

```python
import jax
import jax.numpy as jnp
from jax import lax
from jax.experimental import pallas as pl
from jax.experimental.pallas import tpu as pltpu
from jax.sharding import PartitionSpec as P

BLOCK = 64
SLOTS = 8
NEIGHB = 6
COARSE = 8
LEVELS = 4
FINE_BLOCKS = 8
PAIRS = COARSE // 2
WIDE = 2 * BLOCK
ROWS = COARSE
INTERPRET = False

F32 = jnp.float32
BF16 = jnp.bfloat16
I32 = jnp.int32


def iota(shape, axis):
    return lax.broadcasted_iota(I32, shape, axis)


def product(x, weights):
    return jnp.dot(x, weights, preferred_element_type=F32)


def product_nt(x, weights):
    return lax.dot_general(x, weights, (((1,), (1,)), ((), ())), preferred_element_type=F32)


def split(x):
    high = x.astype(BF16)
    return high, (x - high.astype(F32)).astype(BF16)


def split_rows(x):
    high = x.astype(BF16).astype(F32)
    return jnp.concatenate([high, x - high], axis=0).astype(BF16)


def twice(x):
    return jnp.concatenate([x, x], axis=1)


def own_lanes(pair):
    return iota((ROWS, WIDE), 0) == 2 * pair + iota((ROWS, WIDE), 1) // BLOCK


def spread(values):
    doubled = twice(values)
    return jnp.concatenate([jnp.where(own_lanes(q), doubled, 0.0) for q in range(PAIRS)], axis=1)


def fold(wide):
    kept = sum(jnp.where(own_lanes(q), wide[:, q * WIDE : (q + 1) * WIDE], 0.0) for q in range(PAIRS))
    return kept[:, :BLOCK] + kept[:, BLOCK:]


def squared(error):
    left = (iota((BLOCK, WIDE), 1) < BLOCK).astype(F32).astype(BF16)
    right = (iota((BLOCK, WIDE), 1) >= BLOCK).astype(F32).astype(BF16)
    high, low = split(error)
    weights = jnp.concatenate(
        [
            jnp.concatenate([high * left, high * right], axis=0),
            jnp.concatenate([low * left, low * right], axis=0),
        ],
        axis=1,
    )
    full = product(jnp.concatenate([high, low], axis=0), weights)
    top = full[:BLOCK] + full[BLOCK:]
    return top[:, :WIDE] + top[:, WIDE:]


def operand(errors):
    parts = [split(one) for one in errors]
    return jnp.concatenate(
        [jnp.concatenate([h for h, _ in parts], axis=1), jnp.concatenate([l for _, l in parts], axis=1)],
        axis=0,
    )


def applied(weights, values):
    full = product_nt(split_rows(spread(values)), weights)
    top = full[:ROWS] + full[ROWS:]
    return top[:, :BLOCK] + top[:, BLOCK:]


def smooth(pairs, values):
    eye = iota((BLOCK, WIDE), 0) == iota((BLOCK, WIDE), 1) % BLOCK
    sums = sum(
        jnp.where(own_lanes(q), jnp.sum(jnp.where(eye, pairs[q], 0.0), axis=0, keepdims=True), 0.0)
        for q in range(PAIRS)
    )
    inverse = 1.0 / (jnp.sum(sums, axis=1, keepdims=True) * (1.0 / BLOCK))
    one = eye.astype(F32)
    first = []
    for q in range(PAIRS):
        along = jnp.sum(jnp.where(own_lanes(q), inverse, 0.0), axis=0, keepdims=True)
        first.append(one - pairs[q] * along)
    second = [squared(e) for e in first]
    fourth = [squared(e) for e in second]
    w1, w2, w4 = operand(first), operand(second), operand(fourth)
    y = values
    y = y + applied(w4, applied(w4, y))
    y = y + applied(w4, y)
    y = y + applied(w2, y)
    y = y + applied(w1, y)
    return y * inverse


def picked(index, values):
    return sum(jnp.where(index == x, values[x : x + 1], 0.0) for x in range(COARSE))


def restricted(index, values):
    total = jnp.zeros_like(values)
    for x in range(COARSE):
        row = jnp.sum(jnp.where(index == x, values, 0.0), axis=0, keepdims=True)
        total = total + jnp.where(iota(values.shape, 0) == x, row, 0.0)
    return total


def gathered(maps_ref, doubled):
    return [picked(maps_ref[q], doubled) for q in range(PAIRS)]


def ops_product(ops_ref, tiles):
    stacked = split_rows(jnp.concatenate(tiles, axis=1))
    full = product_nt(stacked, ops_ref[...])
    return fold(full[:ROWS] + full[ROWS:])


def fine_kernel(ops_ref, resid_ref, smooth_ref, rounded_ref):
    pairs = []
    for q in range(PAIRS):
        even = ops_ref[2 * q * BLOCK : (2 * q + 1) * BLOCK, :BLOCK].astype(F32)
        odd = ops_ref[(2 * q + 1) * BLOCK : (2 * q + 2) * BLOCK, :BLOCK].astype(F32)
        pairs.append(jnp.concatenate([even, odd], axis=1))
    out = smooth(pairs, resid_ref[...])
    smooth_ref[...] = out
    rounded_ref[...] = out.astype(BF16)


def tiles_kernel(near_ref, fine_map_ref, maps_ref, ops_ref, cols_ref, tiles_ref, acc_ref):
    acc_ref[...] = jnp.zeros_like(acc_ref)
    left = iota((1, WIDE), 1) < BLOCK
    rows = iota((ROWS, WIDE), 0)
    first_half = iota((ROWS, WIDE), 1) < BLOCK

    def label(j, level):
        value = fine_map_ref[j]
        for step in range(level):
            value = maps_ref[0, step, value]
        return value

    index = [jnp.where(first_half, rows, -1)] + [jnp.full((ROWS, WIDE), -1, I32) for q in range(PAIRS - 1)]
    level_cols = [jnp.zeros((ROWS, WIDE), I32) for level in range(LEVELS)]
    for j in range(FINE_BLOCKS):
        own = [label(j, level) for level in range(LEVELS)]
        others = [near_ref[j, k] for k in range(NEIGHB)]
        for level in range(LEVELS):
            level_cols[level] = jnp.where(rows == j, own[level], level_cols[level])
        for k in range(1, NEIGHB + 1):
            here = (rows == j) & (first_half if k % 2 == 0 else ~first_half)
            index[k // 2] = jnp.where(here, others[k - 1], index[k // 2])
        tiles = [
            ops_ref[j * BLOCK : (j + 1) * BLOCK, q * WIDE : (q + 1) * WIDE].astype(F32) for q in range(PAIRS)
        ]
        for level in range(LEVELS):
            same = [F32(1.0)] + [
                jnp.where(label(others[k], level) == own[level], F32(1.0), F32(0.0)) for k in range(NEIGHB)
            ]
            total = None
            for q in range(PAIRS):
                odd = same[2 * q + 1] if 2 * q + 1 <= NEIGHB else F32(0.0)
                part = tiles[q] * jnp.where(left, same[2 * q], odd)
                total = part if total is None else total + part
            acc_ref[level, own[level]] = acc_ref[level, own[level]] + total
    for q in range(PAIRS):
        cols_ref[q] = index[q]
    for level in range(LEVELS):
        cols_ref[PAIRS + level] = level_cols[level]
        for q in range(PAIRS):
            even, odd = acc_ref[level, 2 * q], acc_ref[level, 2 * q + 1]
            wide_left = iota((BLOCK, WIDE), 1) < BLOCK
            moved = pltpu.roll(jnp.where(wide_left, odd, even), BLOCK, 1)
            tiles_ref[level, q] = jnp.where(wide_left, even, odd) + moved


def store_rows(out_ref, start, values):
    out_ref[start : start + ROWS, :] = twice(values)


SEND0 = ROWS + PAIRS * BLOCK + 2 * BLOCK
SEND1 = ROWS + 2 * BLOCK + BLOCK
SEND2 = ROWS + BLOCK + BLOCK // 2
SEND3 = ROWS + BLOCK // 2


def resid_kernel(ops_ref, resid_ref, rounded_ref, earlier_ref, cols_ref, tiles_ref, fresid_ref, send_ref):
    own = twice(rounded_ref[...].astype(F32))
    before = twice(earlier_ref[...].astype(F32))
    tiles = gathered(cols_ref, own)
    tiles[-1] = jnp.where(iota((ROWS, WIDE), 1) < BLOCK, tiles[-1], before)
    stacked = jnp.concatenate(tiles, axis=1)
    stacked = jnp.concatenate([stacked, jnp.zeros_like(stacked)], axis=0).astype(BF16)
    fresid = resid_ref[...] - fold(product_nt(stacked, ops_ref[...])[:ROWS])
    fresid_ref[...] = fresid
    store_rows(send_ref, 0, restricted(cols_ref[PAIRS][:, :BLOCK], fresid))
    other = 1 - lax.rem(lax.axis_index("gy"), 2)
    for q in range(PAIRS):
        send_ref[ROWS + q * BLOCK : ROWS + (q + 1) * BLOCK, :] = tiles_ref[0, q]
    at = ROWS + PAIRS * BLOCK
    for i in range(2):
        send_ref[at + i * BLOCK : at + (i + 1) * BLOCK, :] = tiles_ref[1, 2 * other + i]


def descend(level, pairs, coarse_rows, ops_ref, cols_ref, fresid_ref, total_ref, fresid_out, total_out):
    out = smooth(pairs, coarse_rows)
    on_fine = picked(cols_ref[PAIRS + level][:, :BLOCK], out)
    total_out[...] = total_ref[...] + on_fine
    fresid = fresid_ref[...] - ops_product(ops_ref, gathered(cols_ref, twice(on_fine)))
    if fresid_out is not None:
        fresid_out[...] = fresid
    return twice(restricted(cols_ref[PAIRS + level + 1][:, :BLOCK], fresid))


def level0_kernel(ops_ref, cols_ref, tiles_ref, sent_ref, got_ref, fresid_ref, total_ref, fresid_out, total_out, send_ref):
    half = lax.rem(lax.axis_index("gy"), 2)
    pairs = [
        tiles_ref[0, q] + got_ref[ROWS + q * BLOCK : ROWS + (q + 1) * BLOCK, :] for q in range(PAIRS)
    ]
    coarse_rows = sent_ref[:ROWS, :BLOCK] + got_ref[:ROWS, :BLOCK]
    at = ROWS + PAIRS * BLOCK
    summed = [tiles_ref[1, 2 * half + i] + got_ref[at + i * BLOCK : at + (i + 1) * BLOCK, :] for i in range(2)]
    rows = descend(0, pairs, coarse_rows, ops_ref, cols_ref, fresid_ref, total_ref, fresid_out, total_out)
    for e in range(4):
        base = e * SEND1
        send_ref[base : base + ROWS, :] = rows
        for i in range(2):
            send_ref[base + ROWS + i * BLOCK : base + ROWS + (i + 1) * BLOCK, :] = summed[i]
        send_ref[base + ROWS + 2 * BLOCK : base + SEND1, :] = tiles_ref[2, e]


def level1_kernel(ops_ref, cols_ref, tiles_ref, got_ref, fresid_ref, total_ref, fresid_out, total_out, send_ref):
    def chunk(e, start, size):
        return got_ref[e * SEND1 + start : e * SEND1 + start + size, :]

    coarse_rows = sum(chunk(e, 0, ROWS) for e in range(4))[:, :BLOCK]
    pairs = []
    for q in range(PAIRS):
        half, i = q // 2, q % 2
        pairs.append(chunk(half, ROWS + i * BLOCK, BLOCK) + chunk(half + 2, ROWS + i * BLOCK, BLOCK))
    summed = sum(chunk(e, ROWS + 2 * BLOCK, BLOCK) for e in range(4))
    rows = descend(1, pairs, coarse_rows, ops_ref, cols_ref, fresid_ref, total_ref, fresid_out, total_out)
    for e in range(8):
        base = e * SEND2
        send_ref[base : base + ROWS, :] = rows
        send_ref[base + ROWS : base + ROWS + BLOCK, :] = summed
        part = BLOCK // 2 * (e % 2)
        send_ref[base + ROWS + BLOCK : base + SEND2, :] = tiles_ref[3, e // 2, part : part + BLOCK // 2, :]


def level2_kernel(ops_ref, cols_ref, got_ref, fresid_ref, total_ref, total_out, send_ref):
    def chunk(e, start, size):
        return got_ref[e * SEND2 + start : e * SEND2 + start + size, :]

    coarse_rows = sum(chunk(e, 0, ROWS) for e in range(8))[:, :BLOCK]
    pairs = [chunk(q, ROWS, BLOCK) + chunk(q + 4, ROWS, BLOCK) for q in range(PAIRS)]
    summed = sum(chunk(e, ROWS + BLOCK, BLOCK // 2) for e in range(8))
    rows = descend(2, pairs, coarse_rows, ops_ref, cols_ref, fresid_ref, total_ref, None, total_out)
    for e in range(16):
        base = e * SEND3
        send_ref[base : base + ROWS, :] = rows
        send_ref[base + ROWS : base + SEND3, :] = summed


def level3_kernel(cols_ref, got_ref, total_ref, out_ref):
    def chunk(e, start, size):
        return got_ref[e * SEND3 + start : e * SEND3 + start + size, :]

    coarse_rows = sum(chunk(e, 0, ROWS) for e in range(16))[:, :BLOCK]
    eighths = [chunk(e, ROWS, BLOCK // 2) + chunk(e + 8, ROWS, BLOCK // 2) for e in range(8)]
    pairs = [jnp.concatenate([eighths[2 * q], eighths[2 * q + 1]], axis=0) for q in range(PAIRS)]
    out = smooth(pairs, coarse_rows)
    out_ref[...] = total_ref[...] + picked(cols_ref[PAIRS + 3][:, :BLOCK], out)


def call(kernel, name, out_shapes, args, scalars=0, scratch=()):
    vmem = pl.BlockSpec(memory_space=pltpu.VMEM)
    smem = pl.BlockSpec(memory_space=pltpu.SMEM)
    return pl.pallas_call(
        kernel,
        name=name,
        out_shape=[jax.ShapeDtypeStruct(shape, kind) for shape, kind in out_shapes],
        in_specs=[smem] * scalars + [vmem] * (len(args) - scalars),
        out_specs=[vmem] * len(out_shapes),
        scratch_shapes=list(scratch),
        interpret=INTERPRET,
    )(*args)


def shared(chunks, size):
    lists = [[g * size + i for i in range(size)] for g in range(lax.axis_size("gy") // size)]
    return lax.all_to_all(chunks, "gy", 0, 0, axis_index_groups=lists, tiled=True)


def on_device(residual, fine_ops, neighbours, fine_map, coarse_maps):
    ops = fine_ops.reshape(FINE_BLOCKS * BLOCK, SLOTS * BLOCK)
    vec = (FINE_BLOCKS, BLOCK)
    fine_smooth, rounded = call(fine_kernel, "fine_smooth", [(vec, F32), (vec, BF16)], [ops, residual])
    earlier = lax.ppermute(rounded, "ta", [(0, 1)])
    cols, tiles = call(
        tiles_kernel,
        "tile_parts",
        [((PAIRS + LEVELS, ROWS, WIDE), I32), ((LEVELS, PAIRS, BLOCK, WIDE), F32)],
        [neighbours, fine_map, coarse_maps, ops],
        scalars=3,
        scratch=[pltpu.VMEM((LEVELS, COARSE, BLOCK, WIDE), F32)],
    )
    fresid, sent = call(
        resid_kernel,
        "fine_resid",
        [(vec, F32), ((SEND0, WIDE), F32)],
        [ops, residual, rounded, earlier, cols, tiles],
    )
    got = lax.ppermute(sent, "gy", [(i, i ^ 1) for i in range(lax.axis_size("gy"))])
    fresid, total, chunks = call(
        level0_kernel,
        "level_0",
        [(vec, F32), (vec, F32), ((4 * SEND1, WIDE), F32)],
        [ops, cols, tiles, sent, got, fresid, fine_smooth],
    )
    got = shared(chunks, 4)
    fresid, total, chunks = call(
        level1_kernel,
        "level_1",
        [(vec, F32), (vec, F32), ((8 * SEND2, WIDE), F32)],
        [ops, cols, tiles, got, fresid, total],
    )
    got = shared(chunks, 8)
    total, chunks = call(
        level2_kernel,
        "level_2",
        [(vec, F32), ((16 * SEND3, WIDE), F32)],
        [ops, cols, got, fresid, total],
    )
    got = shared(chunks, 16)
    (out,) = call(level3_kernel, "level_3", [(vec, F32)], [cols, got, total])
    return out


def solution(mesh):
    return jax.shard_map(
        on_device,
        mesh=mesh,
        in_specs=(
            P(("gx", "gy", "ta"), None),
            P(("gx", "gy", "ta"), None, None),
            P(("gx", "gy", "ta"), None),
            P(("gx", "gy", "ta")),
            P(("gx", "gy", "ta"), None, None),
        ),
        out_specs=P(("gx", "gy", "ta"), None),
        check_vma=False,
    )
```

```python
import jax
import jax.numpy as jnp
from jax import lax
from jax.experimental import pallas as pl
from jax.experimental.pallas import tpu as pltpu
from jax.sharding import PartitionSpec as P

BLOCK = 64
SLOTS = 8
NEIGHB = 6
COARSE = 8
LEVELS = 4
FINE_BLOCKS = 8
PAIRS = COARSE // 2
WIDE = 2 * BLOCK
ROWS = COARSE
GRANT = 12 * 2**20
INTERPRET = False

F32 = jnp.float32
BF16 = jnp.bfloat16
I32 = jnp.int32


def iota(shape, axis):
    return lax.broadcasted_iota(I32, shape, axis)


def product(x, weights):
    return jnp.dot(x, weights, preferred_element_type=F32)


def product_nt(x, weights):
    return lax.dot_general(x, weights, (((1,), (1,)), ((), ())), preferred_element_type=F32)


def split(x):
    high = x.astype(BF16)
    return high, (x - high.astype(F32)).astype(BF16)


def split_rows(x):
    high = x.astype(BF16).astype(F32)
    return jnp.concatenate([high, x - high], axis=0).astype(BF16)


def twice(x):
    return jnp.concatenate([x, x], axis=1)


def own_lanes(pair):
    return iota((ROWS, WIDE), 0) == 2 * pair + iota((ROWS, WIDE), 1) // BLOCK


def spread(values):
    doubled = twice(values)
    return jnp.concatenate([jnp.where(own_lanes(q), doubled, 0.0) for q in range(PAIRS)], axis=1)


def fold(wide):
    kept = sum(jnp.where(own_lanes(q), wide[:, q * WIDE : (q + 1) * WIDE], 0.0) for q in range(PAIRS))
    return kept[:, :BLOCK] + kept[:, BLOCK:]


def squared(error):
    left = (iota((BLOCK, WIDE), 1) < BLOCK).astype(F32).astype(BF16)
    right = (iota((BLOCK, WIDE), 1) >= BLOCK).astype(F32).astype(BF16)
    high, low = split(error)
    weights = jnp.concatenate(
        [
            jnp.concatenate([high * left, high * right], axis=0),
            jnp.concatenate([low * left, low * right], axis=0),
        ],
        axis=1,
    )
    full = product(jnp.concatenate([high, low], axis=0), weights)
    top = full[:BLOCK] + full[BLOCK:]
    return top[:, :WIDE] + top[:, WIDE:]


def operand(errors):
    parts = [split(one) for one in errors]
    return jnp.concatenate(
        [jnp.concatenate([h for h, _ in parts], axis=1), jnp.concatenate([l for _, l in parts], axis=1)],
        axis=0,
    )


def applied(weights, values):
    full = product_nt(split_rows(spread(values)), weights)
    top = full[:ROWS] + full[ROWS:]
    return top[:, :BLOCK] + top[:, BLOCK:]


def smooth(pairs, values):
    eye = iota((BLOCK, WIDE), 0) == iota((BLOCK, WIDE), 1) % BLOCK
    sums = sum(
        jnp.where(own_lanes(q), jnp.sum(jnp.where(eye, pairs[q], 0.0), axis=0, keepdims=True), 0.0)
        for q in range(PAIRS)
    )
    inverse = 1.0 / (jnp.sum(sums, axis=1, keepdims=True) * (1.0 / BLOCK))
    one = eye.astype(F32)
    first = []
    for q in range(PAIRS):
        along = jnp.sum(jnp.where(own_lanes(q), inverse, 0.0), axis=0, keepdims=True)
        first.append(one - pairs[q] * along)
    y = values + applied(operand(first), values)
    second = [squared(e) for e in first]
    y = y + applied(operand(second), y)
    fourth = operand([squared(e) for e in second])
    y = y + applied(fourth, y)
    y = y + applied(fourth, applied(fourth, y))
    return y * inverse


def picked(index, values):
    return sum(jnp.where(index == x, values[x : x + 1], 0.0) for x in range(COARSE))


def restricted(index, values):
    total = jnp.zeros_like(values)
    for x in range(COARSE):
        row = jnp.sum(jnp.where(index == x, values, 0.0), axis=0, keepdims=True)
        total = total + jnp.where(iota(values.shape, 0) == x, row, 0.0)
    return total


def gathered(maps_ref, doubled):
    return [picked(maps_ref[q], doubled) for q in range(PAIRS)]


def ops_product(ops_ref, tiles):
    stacked = split_rows(jnp.concatenate(tiles, axis=1))
    full = product_nt(stacked, ops_ref[...])
    return fold(full[:ROWS] + full[ROWS:])


def fine_kernel(ops_ref, resid_ref, smooth_ref, rounded_ref):
    pairs = []
    for q in range(PAIRS):
        even = ops_ref[2 * q * BLOCK : (2 * q + 1) * BLOCK, :BLOCK].astype(F32)
        odd = ops_ref[(2 * q + 1) * BLOCK : (2 * q + 2) * BLOCK, :BLOCK].astype(F32)
        pairs.append(jnp.concatenate([even, odd], axis=1))
    out = smooth(pairs, resid_ref[...])
    smooth_ref[...] = out
    rounded_ref[...] = out.astype(BF16)


def tiles_kernel(near_ref, fine_map_ref, maps_ref, ops_ref, cols_ref, tiles_ref, acc_ref):
    acc_ref[...] = jnp.zeros_like(acc_ref)
    left = iota((1, WIDE), 1) < BLOCK
    rows = iota((ROWS, WIDE), 0)
    first_half = iota((ROWS, WIDE), 1) < BLOCK

    def label(j, level):
        value = fine_map_ref[j]
        for step in range(level):
            value = maps_ref[step, 0, value]
        return value

    index = [jnp.where(first_half, rows, -1)] + [jnp.full((ROWS, WIDE), -1, I32) for q in range(PAIRS - 1)]
    level_cols = [jnp.zeros((ROWS, WIDE), I32) for level in range(LEVELS)]
    for j in range(FINE_BLOCKS):
        own = [label(j, level) for level in range(LEVELS)]
        others = [near_ref[j, k] for k in range(NEIGHB)]
        for level in range(LEVELS):
            level_cols[level] = jnp.where(rows == j, own[level], level_cols[level])
        for k in range(1, NEIGHB + 1):
            here = (rows == j) & (first_half if k % 2 == 0 else ~first_half)
            index[k // 2] = jnp.where(here, others[k - 1], index[k // 2])
        tiles = [
            ops_ref[j * BLOCK : (j + 1) * BLOCK, q * WIDE : (q + 1) * WIDE].astype(F32) for q in range(PAIRS)
        ]
        for level in range(LEVELS):
            same = [F32(1.0)] + [
                jnp.where(label(others[k], level) == own[level], F32(1.0), F32(0.0)) for k in range(NEIGHB)
            ]
            total = None
            for q in range(PAIRS):
                odd = same[2 * q + 1] if 2 * q + 1 <= NEIGHB else F32(0.0)
                part = tiles[q] * jnp.where(left, same[2 * q], odd)
                total = part if total is None else total + part
            acc_ref[level, own[level]] = acc_ref[level, own[level]] + total
    for q in range(PAIRS):
        cols_ref[q] = index[q]
    for level in range(LEVELS):
        cols_ref[PAIRS + level] = level_cols[level]
        for q in range(PAIRS):
            even, odd = acc_ref[level, 2 * q], acc_ref[level, 2 * q + 1]
            wide_left = iota((BLOCK, WIDE), 1) < BLOCK
            moved = pltpu.roll(jnp.where(wide_left, odd, even), BLOCK, 1)
            tiles_ref[level, q] = jnp.where(wide_left, even, odd) + moved


HEAD = 2 * ROWS
HALF = BLOCK // 2
SEND0 = HEAD + 2 * PAIRS * BLOCK + 2 * BLOCK
SEND1 = HEAD + 2 * BLOCK + BLOCK
SEND2 = HEAD + BLOCK + HALF
SEND3 = HEAD + HALF


def on_diagonal(size, start):
    return iota((size, WIDE), 0) + start == iota((size, WIDE), 1) % BLOCK


def packed(values, parts):
    head = jnp.concatenate([values.astype(BF16).astype(F32), values - values.astype(BF16).astype(F32)], axis=1)
    rows = iota((ROWS, WIDE), 0)
    lows = jnp.zeros((ROWS, WIDE), F32)
    body = []
    for i, (part, start) in enumerate(parts):
        high, low = split(part)
        body.append(high)
        along = jnp.where(on_diagonal(part.shape[0], start), low.astype(F32), 0.0)
        lows = jnp.where(rows == i, jnp.sum(along, axis=0, keepdims=True), lows)
    return jnp.concatenate([jnp.concatenate([head, lows], axis=0).astype(BF16)] + body, axis=0)


def got_rows(ref, base):
    head = ref[base : base + HEAD, :].astype(F32)[:ROWS]
    return head[:, :BLOCK] + head[:, BLOCK:]


def got_part(ref, base, i, at, size, start):
    low = ref[base : base + HEAD, :].astype(F32)[ROWS + i : ROWS + i + 1]
    high = ref[base + at : base + at + size, :].astype(F32)
    return high + jnp.where(on_diagonal(size, start), low, 0.0)


def resid_kernel(ops_ref, resid_ref, rounded_ref, earlier_ref, cols_ref, tiles_ref, fresid_ref, rows_ref, send_ref):
    own = twice(rounded_ref[...].astype(F32))
    before = twice(earlier_ref[...].astype(F32))
    tiles = gathered(cols_ref, own)
    tiles[-1] = jnp.where(iota((ROWS, WIDE), 1) < BLOCK, tiles[-1], before)
    stacked = jnp.concatenate(tiles, axis=1)
    stacked = jnp.concatenate([stacked, jnp.zeros_like(stacked)], axis=0).astype(BF16)
    fresid = resid_ref[...] - fold(product_nt(stacked, ops_ref[...])[:ROWS])
    fresid_ref[...] = fresid
    rows = restricted(cols_ref[PAIRS][:, :BLOCK], fresid)
    rows_ref[...] = rows
    other = 1 - lax.rem(lax.axis_index("gy"), 2)
    send_ref[:HEAD + 2 * BLOCK, :] = packed(rows, [(tiles_ref[1, 2 * other + i], 0) for i in range(2)])
    at = HEAD + 2 * BLOCK
    for q in range(PAIRS):
        high, low = split(tiles_ref[0, q])
        send_ref[at : at + BLOCK, :] = high
        send_ref[at + BLOCK : at + 2 * BLOCK, :] = low
        at += 2 * BLOCK


def descend(level, pairs, coarse_rows, ops_ref, cols_ref, fresid_ref, total_ref, fresid_out, total_out):
    out = smooth(pairs, coarse_rows)
    on_fine = picked(cols_ref[PAIRS + level][:, :BLOCK], out)
    total_out[...] = total_ref[...] + on_fine
    fresid = fresid_ref[...] - ops_product(ops_ref, gathered(cols_ref, twice(on_fine)))
    if fresid_out is not None:
        fresid_out[...] = fresid
    return restricted(cols_ref[PAIRS + level + 1][:, :BLOCK], fresid)


def level0_kernel(ops_ref, cols_ref, tiles_ref, rows_ref, got_ref, fresid_ref, total_ref, fresid_out, total_out, send_ref):
    half = lax.rem(lax.axis_index("gy"), 2)
    at = HEAD + 2 * BLOCK
    pairs = []
    for q in range(PAIRS):
        high = got_ref[at : at + BLOCK, :].astype(F32)
        low = got_ref[at + BLOCK : at + 2 * BLOCK, :].astype(F32)
        pairs.append(tiles_ref[0, q] + high + low)
        at += 2 * BLOCK
    coarse_rows = rows_ref[...] + got_rows(got_ref, 0)
    summed = [tiles_ref[1, 2 * half + i] + got_part(got_ref, 0, i, HEAD + i * BLOCK, BLOCK, 0) for i in range(2)]
    rows = descend(0, pairs, coarse_rows, ops_ref, cols_ref, fresid_ref, total_ref, fresid_out, total_out)
    for e in range(4):
        parts = [(summed[0], 0), (summed[1], 0), (tiles_ref[2, e], 0)]
        send_ref[e * SEND1 : (e + 1) * SEND1, :] = packed(rows, parts)


def level1_kernel(ops_ref, cols_ref, tiles_ref, got_ref, fresid_ref, total_ref, fresid_out, total_out, send_ref):
    coarse_rows = sum(got_rows(got_ref, e * SEND1) for e in range(4))
    pairs = []
    for q in range(PAIRS):
        half, i = q // 2, q % 2
        pairs.append(
            sum(got_part(got_ref, e * SEND1, i, HEAD + i * BLOCK, BLOCK, 0) for e in (half, half + 2))
        )
    summed = sum(got_part(got_ref, e * SEND1, 2, HEAD + 2 * BLOCK, BLOCK, 0) for e in range(4))
    rows = descend(1, pairs, coarse_rows, ops_ref, cols_ref, fresid_ref, total_ref, fresid_out, total_out)
    for e in range(8):
        start = HALF * (e % 2)
        parts = [(summed, 0), (tiles_ref[3, e // 2, start : start + HALF, :], start)]
        send_ref[e * SEND2 : (e + 1) * SEND2, :] = packed(rows, parts)


def level2_kernel(ops_ref, cols_ref, got_ref, fresid_ref, total_ref, total_out, send_ref):
    coarse_rows = sum(got_rows(got_ref, e * SEND2) for e in range(8))
    pairs = [
        sum(got_part(got_ref, e * SEND2, 0, HEAD, BLOCK, 0) for e in (q, q + 4)) for q in range(PAIRS)
    ]
    start = HALF * lax.rem(lax.axis_index("gy"), 2)
    summed = sum(got_part(got_ref, e * SEND2, 1, HEAD + BLOCK, HALF, start) for e in range(8))
    rows = descend(2, pairs, coarse_rows, ops_ref, cols_ref, fresid_ref, total_ref, None, total_out)
    chunk = packed(rows, [(summed, start)])
    for e in range(16):
        send_ref[e * SEND3 : (e + 1) * SEND3, :] = chunk


def level3_kernel(cols_ref, got_ref, total_ref, out_ref):
    coarse_rows = sum(got_rows(got_ref, e * SEND3) for e in range(16))
    eighths = [
        sum(got_part(got_ref, e * SEND3, 0, HEAD, HALF, HALF * (p % 2)) for e in (p, p + 8)) for p in range(8)
    ]
    pairs = [jnp.concatenate([eighths[2 * q], eighths[2 * q + 1]], axis=0) for q in range(PAIRS)]
    out = smooth(pairs, coarse_rows)
    out_ref[...] = total_ref[...] + picked(cols_ref[PAIRS + 3][:, :BLOCK], out)


def call(kernel, name, out_shapes, args, scalars=0, scratch=()):
    vmem = pl.BlockSpec(memory_space=pltpu.VMEM)
    smem = pl.BlockSpec(memory_space=pltpu.SMEM)
    return pl.pallas_call(
        kernel,
        name=name,
        out_shape=[jax.ShapeDtypeStruct(shape, kind) for shape, kind in out_shapes],
        in_specs=[smem] * scalars + [vmem] * (len(args) - scalars),
        out_specs=[vmem] * len(out_shapes),
        scratch_shapes=list(scratch),
        compiler_params=pltpu.CompilerParams(vmem_limit_bytes=GRANT),
        interpret=INTERPRET,
    )(*args)


def shared(chunks, size):
    lists = [[g * size + i for i in range(size)] for g in range(lax.axis_size("gy") // size)]
    return lax.all_to_all(chunks, "gy", 0, 0, axis_index_groups=lists, tiled=True)


def on_device(residual, fine_ops, neighbours, fine_map, coarse_maps):
    ops = fine_ops.reshape(FINE_BLOCKS * BLOCK, SLOTS * BLOCK)
    vec = (FINE_BLOCKS, BLOCK)
    fine_smooth, rounded = call(fine_kernel, "fine_smooth", [(vec, F32), (vec, BF16)], [ops, residual])
    earlier = lax.ppermute(rounded, "ta", [(0, 1)])
    cols, tiles = call(
        tiles_kernel,
        "tile_parts",
        [((PAIRS + LEVELS, ROWS, WIDE), I32), ((LEVELS, PAIRS, BLOCK, WIDE), F32)],
        [neighbours, fine_map, jnp.transpose(coarse_maps, (1, 0, 2)), ops],
        scalars=3,
        scratch=[pltpu.VMEM((LEVELS, COARSE, BLOCK, WIDE), F32)],
    )
    fresid, rows, sent = call(
        resid_kernel,
        "fine_resid",
        [(vec, F32), (vec, F32), ((SEND0, WIDE), BF16)],
        [ops, residual, rounded, earlier, cols, tiles],
    )
    got = lax.ppermute(sent, "gy", [(i, i ^ 1) for i in range(lax.axis_size("gy"))])
    fresid, total, chunks = call(
        level0_kernel,
        "level_0",
        [(vec, F32), (vec, F32), ((4 * SEND1, WIDE), BF16)],
        [ops, cols, tiles, rows, got, fresid, fine_smooth],
    )
    got = shared(chunks, 4)
    fresid, total, chunks = call(
        level1_kernel,
        "level_1",
        [(vec, F32), (vec, F32), ((8 * SEND2, WIDE), BF16)],
        [ops, cols, tiles, got, fresid, total],
    )
    got = shared(chunks, 8)
    total, chunks = call(
        level2_kernel,
        "level_2",
        [(vec, F32), ((16 * SEND3, WIDE), BF16)],
        [ops, cols, got, fresid, total],
    )
    got = shared(chunks, 16)
    (out,) = call(level3_kernel, "level_3", [(vec, F32)], [cols, got, total])
    return out


def solution(mesh):
    return jax.shard_map(
        on_device,
        mesh=mesh,
        in_specs=(
            P(("gx", "gy", "ta"), None),
            P(("gx", "gy", "ta"), None, None),
            P(("gx", "gy", "ta"), None),
            P(("gx", "gy", "ta")),
            P(("gx", "gy", "ta"), None, None),
        ),
        out_specs=P(("gx", "gy", "ta"), None),
        check_vma=False,
    )
```

```python
import jax
import jax.numpy as jnp
from jax import lax
from jax.experimental import pallas as pl
from jax.experimental.pallas import tpu as pltpu
from jax.sharding import PartitionSpec as P

BLOCK = 64
SLOTS = 8
NEIGHB = 6
COARSE = 8
LEVELS = 4
FINE_BLOCKS = 8
PAIRS = COARSE // 2
WIDE = 2 * BLOCK
ROWS = COARSE
GRANT = 12 * 2**20
INTERPRET = False

F32 = jnp.float32
BF16 = jnp.bfloat16
I32 = jnp.int32


def iota(shape, axis):
    return lax.broadcasted_iota(I32, shape, axis)


def product(x, weights):
    return jnp.dot(x, weights, preferred_element_type=F32)


def product_nt(x, weights):
    return lax.dot_general(x, weights, (((1,), (1,)), ((), ())), preferred_element_type=F32)


def split(x):
    high = x.astype(BF16)
    return high, (x - high.astype(F32)).astype(BF16)


def split_rows(x):
    high = x.astype(BF16).astype(F32)
    return jnp.concatenate([high, x - high], axis=0).astype(BF16)


def twice(x):
    return jnp.concatenate([x, x], axis=1)


def own_lanes(pair):
    return iota((ROWS, WIDE), 0) == 2 * pair + iota((ROWS, WIDE), 1) // BLOCK


def spread(values):
    doubled = twice(values)
    return jnp.concatenate([jnp.where(own_lanes(q), doubled, 0.0) for q in range(PAIRS)], axis=1)


def fold(wide):
    kept = sum(jnp.where(own_lanes(q), wide[:, q * WIDE : (q + 1) * WIDE], 0.0) for q in range(PAIRS))
    return kept[:, :BLOCK] + kept[:, BLOCK:]


def squared(error):
    left = (iota((BLOCK, WIDE), 1) < BLOCK).astype(F32).astype(BF16)
    right = (iota((BLOCK, WIDE), 1) >= BLOCK).astype(F32).astype(BF16)
    high, low = split(error)
    weights = jnp.concatenate(
        [
            jnp.concatenate([high * left, high * right], axis=0),
            jnp.concatenate([low * left, low * right], axis=0),
        ],
        axis=1,
    )
    full = product(jnp.concatenate([high, low], axis=0), weights)
    top = full[:BLOCK] + full[BLOCK:]
    return top[:, :WIDE] + top[:, WIDE:]


def operand(errors):
    parts = [split(one) for one in errors]
    return jnp.concatenate(
        [jnp.concatenate([h for h, _ in parts], axis=1), jnp.concatenate([l for _, l in parts], axis=1)],
        axis=0,
    )


def applied(weights, values):
    full = product_nt(split_rows(spread(values)), weights)
    top = full[:ROWS] + full[ROWS:]
    return top[:, :BLOCK] + top[:, BLOCK:]


def smooth(pairs, values):
    eye = iota((BLOCK, WIDE), 0) == iota((BLOCK, WIDE), 1) % BLOCK
    sums = sum(
        jnp.where(own_lanes(q), jnp.sum(jnp.where(eye, pairs[q], 0.0), axis=0, keepdims=True), 0.0)
        for q in range(PAIRS)
    )
    inverse = 1.0 / (jnp.sum(sums, axis=1, keepdims=True) * (1.0 / BLOCK))
    one = eye.astype(F32)
    first = []
    for q in range(PAIRS):
        along = jnp.sum(jnp.where(own_lanes(q), inverse, 0.0), axis=0, keepdims=True)
        first.append(one - pairs[q] * along)
    y = values + applied(operand(first), values)
    second = [squared(e) for e in first]
    y = y + applied(operand(second), y)
    fourth = operand([squared(e) for e in second])
    y = y + applied(fourth, y)
    y = y + applied(fourth, applied(fourth, y))
    return y * inverse


def picked(index, values):
    return sum(jnp.where(index == x, values[x : x + 1], 0.0) for x in range(COARSE))


def restricted(index, values):
    total = jnp.zeros_like(values)
    for x in range(COARSE):
        row = jnp.sum(jnp.where(index == x, values, 0.0), axis=0, keepdims=True)
        total = total + jnp.where(iota(values.shape, 0) == x, row, 0.0)
    return total


def gathered(maps_ref, doubled):
    return [picked(maps_ref[q], doubled) for q in range(PAIRS)]


def ops_product(ops_ref, tiles):
    stacked = split_rows(jnp.concatenate(tiles, axis=1))
    full = product_nt(stacked, ops_ref[...])
    return fold(full[:ROWS] + full[ROWS:])


def fine_kernel(ops_ref, resid_ref, smooth_ref, rounded_ref):
    pairs = []
    for q in range(PAIRS):
        even = ops_ref[2 * q * BLOCK : (2 * q + 1) * BLOCK, :BLOCK].astype(F32)
        odd = ops_ref[(2 * q + 1) * BLOCK : (2 * q + 2) * BLOCK, :BLOCK].astype(F32)
        pairs.append(jnp.concatenate([even, odd], axis=1))
    out = smooth(pairs, resid_ref[...])
    smooth_ref[...] = out
    rounded_ref[...] = out.astype(BF16)


def tiles_kernel(near_ref, fine_map_ref, maps_ref, ops_ref, cols_ref, tiles_ref, acc_ref):
    acc_ref[...] = jnp.zeros_like(acc_ref)
    left = iota((1, WIDE), 1) < BLOCK
    rows = iota((ROWS, WIDE), 0)
    first_half = iota((ROWS, WIDE), 1) < BLOCK

    def label(j, level):
        value = fine_map_ref[j]
        for step in range(level):
            value = maps_ref[step, 0, value]
        return value

    index = [jnp.where(first_half, rows, -1)] + [jnp.full((ROWS, WIDE), -1, I32) for q in range(PAIRS - 1)]
    level_cols = [jnp.zeros((ROWS, WIDE), I32) for level in range(LEVELS)]
    for j in range(FINE_BLOCKS):
        own = [label(j, level) for level in range(LEVELS)]
        others = [near_ref[j, k] for k in range(NEIGHB)]
        for level in range(LEVELS):
            level_cols[level] = jnp.where(rows == j, own[level], level_cols[level])
        for k in range(1, NEIGHB + 1):
            here = (rows == j) & (first_half if k % 2 == 0 else ~first_half)
            index[k // 2] = jnp.where(here, others[k - 1], index[k // 2])
        tiles = [
            ops_ref[j * BLOCK : (j + 1) * BLOCK, q * WIDE : (q + 1) * WIDE].astype(F32) for q in range(PAIRS)
        ]
        for level in range(LEVELS):
            same = [F32(1.0)] + [
                jnp.where(label(others[k], level) == own[level], F32(1.0), F32(0.0)) for k in range(NEIGHB)
            ]
            total = None
            for q in range(PAIRS):
                odd = same[2 * q + 1] if 2 * q + 1 <= NEIGHB else F32(0.0)
                part = tiles[q] * jnp.where(left, same[2 * q], odd)
                total = part if total is None else total + part
            acc_ref[level, own[level]] = acc_ref[level, own[level]] + total
    for q in range(PAIRS):
        cols_ref[q] = index[q]
    for level in range(LEVELS):
        cols_ref[PAIRS + level] = level_cols[level]
        for q in range(PAIRS):
            even, odd = acc_ref[level, 2 * q], acc_ref[level, 2 * q + 1]
            wide_left = iota((BLOCK, WIDE), 1) < BLOCK
            moved = pltpu.roll(jnp.where(wide_left, odd, even), BLOCK, 1)
            tiles_ref[level, q] = jnp.where(wide_left, even, odd) + moved


HEAD = 2 * ROWS
HALF = BLOCK // 2
SEND0 = HEAD + 2 * PAIRS * BLOCK + 2 * BLOCK
SEND1 = HEAD + 2 * BLOCK + BLOCK
SEND2 = HEAD + BLOCK + HALF
SEND3 = HEAD + HALF


def on_diagonal(size, start):
    return iota((size, WIDE), 0) + start == iota((size, WIDE), 1) % BLOCK


def packed(values, parts):
    head = jnp.concatenate([values.astype(BF16).astype(F32), values - values.astype(BF16).astype(F32)], axis=1)
    rows = iota((ROWS, WIDE), 0)
    lows = jnp.zeros((ROWS, WIDE), F32)
    body = []
    for i, (part, start) in enumerate(parts):
        high, low = split(part)
        body.append(high)
        along = jnp.where(on_diagonal(part.shape[0], start), low.astype(F32), 0.0)
        lows = jnp.where(rows == i, jnp.sum(along, axis=0, keepdims=True), lows)
    return jnp.concatenate([jnp.concatenate([head, lows], axis=0).astype(BF16)] + body, axis=0)


def got_rows(ref, base):
    head = ref[base : base + HEAD, :].astype(F32)[:ROWS]
    return head[:, :BLOCK] + head[:, BLOCK:]


def got_part(ref, base, i, at, size, start):
    low = ref[base : base + HEAD, :].astype(F32)[ROWS + i : ROWS + i + 1]
    high = ref[base + at : base + at + size, :].astype(F32)
    return high + jnp.where(on_diagonal(size, start), low, 0.0)


def resid_kernel(ops_ref, resid_ref, rounded_ref, earlier_ref, cols_ref, tiles_ref, fresid_ref, rows_ref, send_ref):
    own = twice(rounded_ref[...].astype(F32))
    before = twice(earlier_ref[...].astype(F32))
    tiles = gathered(cols_ref, own)
    tiles[-1] = jnp.where(iota((ROWS, WIDE), 1) < BLOCK, tiles[-1], before)
    stacked = jnp.concatenate(tiles, axis=1)
    stacked = jnp.concatenate([stacked, jnp.zeros_like(stacked)], axis=0).astype(BF16)
    fresid = resid_ref[...] - fold(product_nt(stacked, ops_ref[...])[:ROWS])
    fresid_ref[...] = fresid
    rows = restricted(cols_ref[PAIRS][:, :BLOCK], fresid)
    rows_ref[...] = rows
    other = 1 - lax.rem(lax.axis_index("gy"), 2)
    send_ref[:HEAD + 2 * BLOCK, :] = packed(rows, [(tiles_ref[1, 2 * other + i], 0) for i in range(2)])
    at = HEAD + 2 * BLOCK
    for q in range(PAIRS):
        high, low = split(tiles_ref[0, q])
        send_ref[at : at + BLOCK, :] = high
        send_ref[at + BLOCK : at + 2 * BLOCK, :] = low
        at += 2 * BLOCK


def descend(level, pairs, coarse_rows, ops_ref, cols_ref, fresid_ref, total_ref, fresid_out, total_out):
    out = smooth(pairs, coarse_rows)
    on_fine = picked(cols_ref[PAIRS + level][:, :BLOCK], out)
    total_out[...] = total_ref[...] + on_fine
    fresid = fresid_ref[...] - ops_product(ops_ref, gathered(cols_ref, twice(on_fine)))
    if fresid_out is not None:
        fresid_out[...] = fresid
    return restricted(cols_ref[PAIRS + level + 1][:, :BLOCK], fresid)


def level0_kernel(ops_ref, cols_ref, tiles_ref, rows_ref, got_ref, fresid_ref, total_ref, fresid_out, total_out, send_ref):
    half = lax.rem(lax.axis_index("gy"), 2)
    at = HEAD + 2 * BLOCK
    pairs = []
    for q in range(PAIRS):
        high = got_ref[at : at + BLOCK, :].astype(F32)
        low = got_ref[at + BLOCK : at + 2 * BLOCK, :].astype(F32)
        pairs.append(tiles_ref[0, q] + high + low)
        at += 2 * BLOCK
    coarse_rows = rows_ref[...] + got_rows(got_ref, 0)
    summed = [tiles_ref[1, 2 * half + i] + got_part(got_ref, 0, i, HEAD + i * BLOCK, BLOCK, 0) for i in range(2)]
    rows = descend(0, pairs, coarse_rows, ops_ref, cols_ref, fresid_ref, total_ref, fresid_out, total_out)
    for e in range(4):
        parts = [(summed[0], 0), (summed[1], 0), (tiles_ref[2, e], 0)]
        send_ref[e * SEND1 : (e + 1) * SEND1, :] = packed(rows, parts)


def level1_kernel(ops_ref, cols_ref, tiles_ref, got_ref, fresid_ref, total_ref, fresid_out, total_out, send_ref):
    coarse_rows = sum(got_rows(got_ref, e * SEND1) for e in range(4))
    pairs = []
    for q in range(PAIRS):
        half, i = q // 2, q % 2
        pairs.append(
            sum(got_part(got_ref, e * SEND1, i, HEAD + i * BLOCK, BLOCK, 0) for e in (half, half + 2))
        )
    summed = sum(got_part(got_ref, e * SEND1, 2, HEAD + 2 * BLOCK, BLOCK, 0) for e in range(4))
    rows = descend(1, pairs, coarse_rows, ops_ref, cols_ref, fresid_ref, total_ref, fresid_out, total_out)
    for e in range(8):
        start = HALF * (e % 2)
        parts = [(summed, 0), (tiles_ref[3, e // 2, start : start + HALF, :], start)]
        send_ref[e * SEND2 : (e + 1) * SEND2, :] = packed(rows, parts)


def level2_kernel(ops_ref, cols_ref, got_ref, fresid_ref, total_ref, total_out, rows_out, part_out, send_ref):
    coarse_rows = sum(got_rows(got_ref, e * SEND2) for e in range(8))
    pairs = [
        sum(got_part(got_ref, e * SEND2, 0, HEAD, BLOCK, 0) for e in (q, q + 4)) for q in range(PAIRS)
    ]
    start = HALF * lax.rem(lax.axis_index("gy"), 2)
    summed = sum(got_part(got_ref, e * SEND2, 1, HEAD + BLOCK, HALF, start) for e in range(8))
    rows = descend(2, pairs, coarse_rows, ops_ref, cols_ref, fresid_ref, total_ref, None, total_out)
    rows_out[...] = rows
    part_out[...] = summed
    send_ref[...] = packed(rows, [(summed, start)])


def join_kernel(rows_ref, part_ref, got_ref, send_ref):
    start = HALF * lax.rem(lax.axis_index("gy"), 2)
    rows = rows_ref[...] + got_rows(got_ref, 0)
    chunk = packed(rows, [(part_ref[...] + got_part(got_ref, 0, 0, HEAD, HALF, start), start)])
    for e in range(8):
        send_ref[e * SEND3 : (e + 1) * SEND3, :] = chunk


def level3_kernel(cols_ref, got_ref, total_ref, out_ref):
    coarse_rows = sum(got_rows(got_ref, e * SEND3) for e in range(8))
    eighths = [got_part(got_ref, e * SEND3, 0, HEAD, HALF, HALF * (e % 2)) for e in range(8)]
    pairs = [jnp.concatenate([eighths[2 * q], eighths[2 * q + 1]], axis=0) for q in range(PAIRS)]
    out = smooth(pairs, coarse_rows)
    out_ref[...] = total_ref[...] + picked(cols_ref[PAIRS + 3][:, :BLOCK], out)


def call(kernel, name, out_shapes, args, scalars=0, scratch=()):
    vmem = pl.BlockSpec(memory_space=pltpu.VMEM)
    smem = pl.BlockSpec(memory_space=pltpu.SMEM)
    return pl.pallas_call(
        kernel,
        name=name,
        out_shape=[jax.ShapeDtypeStruct(shape, kind) for shape, kind in out_shapes],
        in_specs=[smem] * scalars + [vmem] * (len(args) - scalars),
        out_specs=[vmem] * len(out_shapes),
        scratch_shapes=list(scratch),
        compiler_params=pltpu.CompilerParams(vmem_limit_bytes=GRANT),
        interpret=INTERPRET,
    )(*args)


def shared(chunks, size):
    lists = [[g * size + i for i in range(size)] for g in range(lax.axis_size("gy") // size)]
    return lax.all_to_all(chunks, "gy", 0, 0, axis_index_groups=lists, tiled=True)


def crossed(value, distance):
    return lax.ppermute(value, "gy", [(i, i ^ distance) for i in range(lax.axis_size("gy"))])


def on_device(residual, fine_ops, neighbours, fine_map, coarse_maps):
    ops = fine_ops.reshape(FINE_BLOCKS * BLOCK, SLOTS * BLOCK)
    vec = (FINE_BLOCKS, BLOCK)
    fine_smooth, rounded = call(fine_kernel, "fine_smooth", [(vec, F32), (vec, BF16)], [ops, residual])
    earlier = lax.ppermute(rounded, "ta", [(0, 1)])
    cols, tiles = call(
        tiles_kernel,
        "tile_parts",
        [((PAIRS + LEVELS, ROWS, WIDE), I32), ((LEVELS, PAIRS, BLOCK, WIDE), F32)],
        [neighbours, fine_map, jnp.transpose(coarse_maps, (1, 0, 2)), ops],
        scalars=3,
        scratch=[pltpu.VMEM((LEVELS, COARSE, BLOCK, WIDE), F32)],
    )
    fresid, rows, sent = call(
        resid_kernel,
        "fine_resid",
        [(vec, F32), (vec, F32), ((SEND0, WIDE), BF16)],
        [ops, residual, rounded, earlier, cols, tiles],
    )
    got = crossed(sent, 1)
    fresid, total, chunks = call(
        level0_kernel,
        "level_0",
        [(vec, F32), (vec, F32), ((4 * SEND1, WIDE), BF16)],
        [ops, cols, tiles, rows, got, fresid, fine_smooth],
    )
    got = shared(chunks, 4)
    fresid, total, chunks = call(
        level1_kernel,
        "level_1",
        [(vec, F32), (vec, F32), ((8 * SEND2, WIDE), BF16)],
        [ops, cols, tiles, got, fresid, total],
    )
    got = shared(chunks, 8)
    total, rows, part, sent = call(
        level2_kernel,
        "level_2",
        [(vec, F32), (vec, F32), ((HALF, WIDE), F32), ((SEND3, WIDE), BF16)],
        [ops, cols, got, fresid, total],
    )
    got = crossed(sent, 8)
    (chunks,) = call(join_kernel, "join", [((8 * SEND3, WIDE), BF16)], [rows, part, got])
    got = shared(chunks, 8)
    (out,) = call(level3_kernel, "level_3", [(vec, F32)], [cols, got, total])
    return out


def solution(mesh):
    return jax.shard_map(
        on_device,
        mesh=mesh,
        in_specs=(
            P(("gx", "gy", "ta"), None),
            P(("gx", "gy", "ta"), None, None),
            P(("gx", "gy", "ta"), None),
            P(("gx", "gy", "ta")),
            P(("gx", "gy", "ta"), None, None),
        ),
        out_specs=P(("gx", "gy", "ta"), None),
        check_vma=False,
    )
```

```python
import jax
import jax.numpy as jnp
from jax import lax
from jax.experimental import pallas as pl
from jax.experimental.pallas import tpu as pltpu
from jax.sharding import PartitionSpec as P

BLOCK = 64
SLOTS = 8
NEIGHB = 6
COARSE = 8
LEVELS = 4
FINE_BLOCKS = 8
PAIRS = COARSE // 2
WIDE = 2 * BLOCK
ROWS = COARSE
GRANT = 12 * 2**20
FIRST_GRANT = 60 * 2**20
INTERPRET = False

F32 = jnp.float32
BF16 = jnp.bfloat16
I32 = jnp.int32


def iota(shape, axis):
    return lax.broadcasted_iota(I32, shape, axis)


def product(x, weights):
    return jnp.dot(x, weights, preferred_element_type=F32)


def product_nt(x, weights):
    return lax.dot_general(x, weights, (((1,), (1,)), ((), ())), preferred_element_type=F32)


def split(x):
    high = x.astype(BF16)
    return high, (x - high.astype(F32)).astype(BF16)


def split_rows(x):
    high = x.astype(BF16).astype(F32)
    return jnp.concatenate([high, x - high], axis=0).astype(BF16)


def twice(x):
    return jnp.concatenate([x, x], axis=1)


def own_lanes(pair):
    return iota((ROWS, WIDE), 0) == 2 * pair + iota((ROWS, WIDE), 1) // BLOCK


def spread(values):
    doubled = twice(values)
    return jnp.concatenate([jnp.where(own_lanes(q), doubled, 0.0) for q in range(PAIRS)], axis=1)


def fold(wide):
    kept = sum(jnp.where(own_lanes(q), wide[:, q * WIDE : (q + 1) * WIDE], 0.0) for q in range(PAIRS))
    return kept[:, :BLOCK] + kept[:, BLOCK:]


def squared(error):
    left = (iota((BLOCK, WIDE), 1) < BLOCK).astype(F32).astype(BF16)
    right = (iota((BLOCK, WIDE), 1) >= BLOCK).astype(F32).astype(BF16)
    high, low = split(error)
    weights = jnp.concatenate(
        [
            jnp.concatenate([high * left, high * right], axis=0),
            jnp.concatenate([low * left, low * right], axis=0),
        ],
        axis=1,
    )
    full = product(jnp.concatenate([high, low], axis=0), weights)
    top = full[:BLOCK] + full[BLOCK:]
    return top[:, :WIDE] + top[:, WIDE:]


def operand(errors):
    parts = [split(one) for one in errors]
    return jnp.concatenate(
        [jnp.concatenate([h for h, _ in parts], axis=1), jnp.concatenate([l for _, l in parts], axis=1)],
        axis=0,
    )


def applied(weights, values):
    full = product_nt(split_rows(spread(values)), weights)
    top = full[:ROWS] + full[ROWS:]
    return top[:, :BLOCK] + top[:, BLOCK:]


def smooth(pairs, values):
    eye = iota((BLOCK, WIDE), 0) == iota((BLOCK, WIDE), 1) % BLOCK
    sums = sum(
        jnp.where(own_lanes(q), jnp.sum(jnp.where(eye, pairs[q], 0.0), axis=0, keepdims=True), 0.0)
        for q in range(PAIRS)
    )
    inverse = 1.0 / (jnp.sum(sums, axis=1, keepdims=True) * (1.0 / BLOCK))
    one = eye.astype(F32)
    first = []
    for q in range(PAIRS):
        along = jnp.sum(jnp.where(own_lanes(q), inverse, 0.0), axis=0, keepdims=True)
        first.append(one - pairs[q] * along)
    y = values + applied(operand(first), values)
    second = [squared(e) for e in first]
    y = y + applied(operand(second), y)
    fourth = [squared(e) for e in second]
    y = y + applied(operand(fourth), y)
    y = y + applied(operand([squared(e) for e in fourth]), y)
    return y * inverse


def picked(index, values):
    return sum(jnp.where(index == x, values[x : x + 1], 0.0) for x in range(COARSE))


def restricted(index, values):
    total = jnp.zeros_like(values)
    for x in range(COARSE):
        row = jnp.sum(jnp.where(index == x, values, 0.0), axis=0, keepdims=True)
        total = total + jnp.where(iota(values.shape, 0) == x, row, 0.0)
    return total


def gathered(maps_ref, doubled):
    return [picked(maps_ref[q], doubled) for q in range(PAIRS)]


def ops_product(ops_ref, tiles):
    stacked = split_rows(jnp.concatenate(tiles, axis=1))
    full = product_nt(stacked, ops_ref[...])
    return fold(full[:ROWS] + full[ROWS:])


def fine_kernel(ops_hbm, resid_hbm, smooth_ref, rounded_ref, diag_ref, resid_ref, diag_sem, resid_sem):
    diag_copy = pltpu.make_async_copy(ops_hbm.at[:, :WIDE], diag_ref, diag_sem)
    resid_copy = pltpu.make_async_copy(resid_hbm, resid_ref, resid_sem)
    diag_copy.start()
    resid_copy.start()
    diag_copy.wait()
    resid_copy.wait()
    pairs = []
    for q in range(PAIRS):
        even = diag_ref[2 * q * BLOCK : (2 * q + 1) * BLOCK, :BLOCK].astype(F32)
        odd = diag_ref[(2 * q + 1) * BLOCK : (2 * q + 2) * BLOCK, :BLOCK].astype(F32)
        pairs.append(jnp.concatenate([even, odd], axis=1))
    out = smooth(pairs, resid_ref[...])
    smooth_ref[...] = out
    rounded_ref[...] = out.astype(BF16)


def tiles_kernel(near_ref, fine_map_ref, maps_ref, ops_ref, cols_ref, tiles_ref, acc_ref):
    acc_ref[...] = jnp.zeros_like(acc_ref)
    left = iota((1, WIDE), 1) < BLOCK
    rows = iota((ROWS, WIDE), 0)
    first_half = iota((ROWS, WIDE), 1) < BLOCK

    def label(j, level):
        value = fine_map_ref[j]
        for step in range(level):
            value = maps_ref[step, 0, value]
        return value

    index = [jnp.where(first_half, rows, -1)] + [jnp.full((ROWS, WIDE), -1, I32) for q in range(PAIRS - 1)]
    level_cols = [jnp.zeros((ROWS, WIDE), I32) for level in range(LEVELS)]
    for j in range(FINE_BLOCKS):
        own = [label(j, level) for level in range(LEVELS)]
        others = [near_ref[j, k] for k in range(NEIGHB)]
        for level in range(LEVELS):
            level_cols[level] = jnp.where(rows == j, own[level], level_cols[level])
        for k in range(1, NEIGHB + 1):
            here = (rows == j) & (first_half if k % 2 == 0 else ~first_half)
            index[k // 2] = jnp.where(here, others[k - 1], index[k // 2])
        tiles = [
            ops_ref[j * BLOCK : (j + 1) * BLOCK, q * WIDE : (q + 1) * WIDE].astype(F32) for q in range(PAIRS)
        ]
        for level in range(LEVELS):
            same = [F32(1.0)] + [
                jnp.where(label(others[k], level) == own[level], F32(1.0), F32(0.0)) for k in range(NEIGHB)
            ]
            total = None
            for q in range(PAIRS):
                odd = same[2 * q + 1] if 2 * q + 1 <= NEIGHB else F32(0.0)
                part = tiles[q] * jnp.where(left, same[2 * q], odd)
                total = part if total is None else total + part
            acc_ref[level, own[level]] = acc_ref[level, own[level]] + total
    for q in range(PAIRS):
        cols_ref[q] = index[q]
    for level in range(LEVELS):
        cols_ref[PAIRS + level] = level_cols[level]
        for q in range(PAIRS):
            even, odd = acc_ref[level, 2 * q], acc_ref[level, 2 * q + 1]
            wide_left = iota((BLOCK, WIDE), 1) < BLOCK
            moved = pltpu.roll(jnp.where(wide_left, odd, even), BLOCK, 1)
            tiles_ref[level, q] = jnp.where(wide_left, even, odd) + moved


HEAD = 2 * ROWS
HALF = BLOCK // 2
SEND0 = HEAD + PAIRS * BLOCK + 2 * BLOCK
SEND1 = HEAD + 2 * BLOCK + BLOCK
SEND2 = HEAD + BLOCK + HALF
SEND3 = HEAD + HALF


def on_diagonal(size, start):
    return iota((size, WIDE), 0) + start == iota((size, WIDE), 1) % BLOCK


def packed(values, parts):
    head = jnp.concatenate([values.astype(BF16).astype(F32), values - values.astype(BF16).astype(F32)], axis=1)
    rows = iota((ROWS, WIDE), 0)
    lows = jnp.zeros((ROWS, WIDE), F32)
    body = []
    for i, (part, start) in enumerate(parts):
        high, low = split(part)
        body.append(high)
        along = jnp.where(on_diagonal(part.shape[0], start), low.astype(F32), 0.0)
        lows = jnp.where(rows == i, jnp.sum(along, axis=0, keepdims=True), lows)
    return jnp.concatenate([jnp.concatenate([head, lows], axis=0).astype(BF16)] + body, axis=0)


def got_rows(ref, base):
    head = ref[base : base + HEAD, :].astype(F32)[:ROWS]
    return head[:, :BLOCK] + head[:, BLOCK:]


def got_part(ref, base, i, at, size, start):
    low = ref[base : base + HEAD, :].astype(F32)[ROWS + i : ROWS + i + 1]
    high = ref[base + at : base + at + size, :].astype(F32)
    return high + jnp.where(on_diagonal(size, start), low, 0.0)


def resid_kernel(ops_ref, resid_ref, rounded_ref, earlier_ref, cols_ref, tiles_ref, fresid_ref, rows_ref, send_ref):
    own = twice(rounded_ref[...].astype(F32))
    before = twice(earlier_ref[...].astype(F32))
    tiles = gathered(cols_ref, own)
    tiles[-1] = jnp.where(iota((ROWS, WIDE), 1) < BLOCK, tiles[-1], before)
    stacked = jnp.concatenate(tiles, axis=1)
    stacked = jnp.concatenate([stacked, jnp.zeros_like(stacked)], axis=0).astype(BF16)
    fresid = resid_ref[...] - fold(product_nt(stacked, ops_ref[...])[:ROWS])
    fresid_ref[...] = fresid
    rows = restricted(cols_ref[PAIRS][:, :BLOCK], fresid)
    rows_ref[...] = rows
    other = 1 - lax.rem(lax.axis_index("gy"), 2)
    parts = [(tiles_ref[0, q], 0) for q in range(PAIRS)] + [(tiles_ref[1, 2 * other + i], 0) for i in range(2)]
    send_ref[...] = packed(rows, parts)


def descend(level, pairs, coarse_rows, ops_ref, cols_ref, fresid_ref, total_ref, fresid_out, total_out):
    out = smooth(pairs, coarse_rows)
    on_fine = picked(cols_ref[PAIRS + level][:, :BLOCK], out)
    total_out[...] = total_ref[...] + on_fine
    fresid = fresid_ref[...] - ops_product(ops_ref, gathered(cols_ref, twice(on_fine)))
    if fresid_out is not None:
        fresid_out[...] = fresid
    return restricted(cols_ref[PAIRS + level + 1][:, :BLOCK], fresid)


def level0_kernel(ops_ref, cols_ref, tiles_ref, rows_ref, got_ref, fresid_ref, total_ref, fresid_out, total_out, send_ref):
    half = lax.rem(lax.axis_index("gy"), 2)
    received = [got_part(got_ref, 0, i, HEAD + i * BLOCK, BLOCK, 0) for i in range(PAIRS + 2)]
    pairs = [tiles_ref[0, q] + received[q] for q in range(PAIRS)]
    coarse_rows = rows_ref[...] + got_rows(got_ref, 0)
    summed = [tiles_ref[1, 2 * half + i] + received[PAIRS + i] for i in range(2)]
    rows = descend(0, pairs, coarse_rows, ops_ref, cols_ref, fresid_ref, total_ref, fresid_out, total_out)
    for e in range(4):
        parts = [(summed[0], 0), (summed[1], 0), (tiles_ref[2, e], 0)]
        send_ref[e * SEND1 : (e + 1) * SEND1, :] = packed(rows, parts)


def level1_kernel(ops_ref, cols_ref, tiles_ref, got_ref, fresid_ref, total_ref, fresid_out, total_out, send_ref):
    coarse_rows = sum(got_rows(got_ref, e * SEND1) for e in range(4))
    pairs = []
    for q in range(PAIRS):
        half, i = q // 2, q % 2
        pairs.append(
            sum(got_part(got_ref, e * SEND1, i, HEAD + i * BLOCK, BLOCK, 0) for e in (half, half + 2))
        )
    summed = sum(got_part(got_ref, e * SEND1, 2, HEAD + 2 * BLOCK, BLOCK, 0) for e in range(4))
    rows = descend(1, pairs, coarse_rows, ops_ref, cols_ref, fresid_ref, total_ref, fresid_out, total_out)
    for e in range(8):
        start = HALF * (e % 2)
        parts = [(summed, 0), (tiles_ref[3, e // 2, start : start + HALF, :], start)]
        send_ref[e * SEND2 : (e + 1) * SEND2, :] = packed(rows, parts)


def level2_kernel(ops_ref, cols_ref, got_ref, fresid_ref, total_ref, total_out, rows_out, part_out, send_ref):
    coarse_rows = sum(got_rows(got_ref, e * SEND2) for e in range(8))
    pairs = [
        sum(got_part(got_ref, e * SEND2, 0, HEAD, BLOCK, 0) for e in (q, q + 4)) for q in range(PAIRS)
    ]
    start = HALF * lax.rem(lax.axis_index("gy"), 2)
    summed = sum(got_part(got_ref, e * SEND2, 1, HEAD + BLOCK, HALF, start) for e in range(8))
    rows = descend(2, pairs, coarse_rows, ops_ref, cols_ref, fresid_ref, total_ref, None, total_out)
    rows_out[...] = rows
    part_out[...] = summed
    send_ref[...] = packed(rows, [(summed, start)])


def join_kernel(rows_ref, part_ref, got_ref, send_ref):
    start = HALF * lax.rem(lax.axis_index("gy"), 2)
    rows = rows_ref[...] + got_rows(got_ref, 0)
    chunk = packed(rows, [(part_ref[...] + got_part(got_ref, 0, 0, HEAD, HALF, start), start)])
    for e in range(8):
        send_ref[e * SEND3 : (e + 1) * SEND3, :] = chunk


def level3_kernel(cols_ref, got_ref, total_ref, out_ref):
    coarse_rows = sum(got_rows(got_ref, e * SEND3) for e in range(8))
    eighths = [got_part(got_ref, e * SEND3, 0, HEAD, HALF, HALF * (e % 2)) for e in range(8)]
    pairs = [jnp.concatenate([eighths[2 * q], eighths[2 * q + 1]], axis=0) for q in range(PAIRS)]
    out = smooth(pairs, coarse_rows)
    out_ref[...] = total_ref[...] + picked(cols_ref[PAIRS + 3][:, :BLOCK], out)


def call(kernel, name, out_shapes, args, scalars=0, scratch=(), outside=0, grant=GRANT):
    hbm = pl.BlockSpec(memory_space=pltpu.HBM)
    vmem = pl.BlockSpec(memory_space=pltpu.VMEM)
    smem = pl.BlockSpec(memory_space=pltpu.SMEM)
    return pl.pallas_call(
        kernel,
        name=name,
        out_shape=[jax.ShapeDtypeStruct(shape, kind) for shape, kind in out_shapes],
        in_specs=[smem] * scalars + [hbm] * outside + [vmem] * (len(args) - scalars - outside),
        out_specs=[vmem] * len(out_shapes),
        scratch_shapes=list(scratch),
        compiler_params=pltpu.CompilerParams(vmem_limit_bytes=grant),
        interpret=INTERPRET,
    )(*args)


def shared(chunks, size):
    lists = [[g * size + i for i in range(size)] for g in range(lax.axis_size("gy") // size)]
    return lax.all_to_all(chunks, "gy", 0, 0, axis_index_groups=lists, tiled=True)


def crossed(value, distance):
    return lax.ppermute(value, "gy", [(i, i ^ distance) for i in range(lax.axis_size("gy"))])


def on_device(residual, fine_ops, neighbours, fine_map, coarse_maps):
    ops = fine_ops.reshape(FINE_BLOCKS * BLOCK, SLOTS * BLOCK)
    vec = (FINE_BLOCKS, BLOCK)
    fine_smooth, rounded = call(
        fine_kernel,
        "fine_smooth",
        [(vec, F32), (vec, BF16)],
        [ops, residual],
        outside=2,
        grant=FIRST_GRANT,
        scratch=[
            pltpu.VMEM((FINE_BLOCKS * BLOCK, WIDE), BF16),
            pltpu.VMEM(vec, F32),
            pltpu.SemaphoreType.DMA,
            pltpu.SemaphoreType.DMA,
        ],
    )
    earlier = lax.ppermute(rounded, "ta", [(0, 1)])
    cols, tiles = call(
        tiles_kernel,
        "tile_parts",
        [((PAIRS + LEVELS, ROWS, WIDE), I32), ((LEVELS, PAIRS, BLOCK, WIDE), F32)],
        [neighbours, fine_map, jnp.transpose(coarse_maps, (1, 0, 2)), ops],
        scalars=3,
        scratch=[pltpu.VMEM((LEVELS, COARSE, BLOCK, WIDE), F32)],
    )
    fresid, rows, sent = call(
        resid_kernel,
        "fine_resid",
        [(vec, F32), (vec, F32), ((SEND0, WIDE), BF16)],
        [ops, residual, rounded, earlier, cols, tiles],
    )
    got = crossed(sent, 1)
    fresid, total, chunks = call(
        level0_kernel,
        "level_0",
        [(vec, F32), (vec, F32), ((4 * SEND1, WIDE), BF16)],
        [ops, cols, tiles, rows, got, fresid, fine_smooth],
    )
    got = shared(chunks, 4)
    fresid, total, chunks = call(
        level1_kernel,
        "level_1",
        [(vec, F32), (vec, F32), ((8 * SEND2, WIDE), BF16)],
        [ops, cols, tiles, got, fresid, total],
    )
    got = shared(chunks, 8)
    total, rows, part, sent = call(
        level2_kernel,
        "level_2",
        [(vec, F32), (vec, F32), ((HALF, WIDE), F32), ((SEND3, WIDE), BF16)],
        [ops, cols, got, fresid, total],
    )
    got = crossed(sent, 8)
    (chunks,) = call(join_kernel, "join", [((8 * SEND3, WIDE), BF16)], [rows, part, got])
    got = shared(chunks, 8)
    (out,) = call(level3_kernel, "level_3", [(vec, F32)], [cols, got, total])
    return out


def solution(mesh):
    return jax.shard_map(
        on_device,
        mesh=mesh,
        in_specs=(
            P(("gx", "gy", "ta"), None),
            P(("gx", "gy", "ta"), None, None),
            P(("gx", "gy", "ta"), None),
            P(("gx", "gy", "ta")),
            P(("gx", "gy", "ta"), None, None),
        ),
        out_specs=P(("gx", "gy", "ta"), None),
        check_vma=False,
    )
```

```python
import jax
import jax.numpy as jnp
from jax import lax
from jax.experimental import pallas as pl
from jax.experimental.pallas import tpu as pltpu
from jax.sharding import PartitionSpec as P

BLOCK = 64
SLOTS = 8
NEIGHB = 6
COARSE = 8
LEVELS = 4
FINE_BLOCKS = 8
PAIRS = COARSE // 2
WIDE = 2 * BLOCK
ROWS = COARSE
GRANT = 12 * 2**20
FIRST_GRANT = 55224 * 2**10
INTERPRET = False

F32 = jnp.float32
BF16 = jnp.bfloat16
I32 = jnp.int32


def iota(shape, axis):
    return lax.broadcasted_iota(I32, shape, axis)


def product(x, weights):
    return jnp.dot(x, weights, preferred_element_type=F32)


def product_nt(x, weights):
    return lax.dot_general(x, weights, (((1,), (1,)), ((), ())), preferred_element_type=F32)


def split(x):
    high = x.astype(BF16)
    return high, (x - high.astype(F32)).astype(BF16)


def split_rows(x):
    high = x.astype(BF16).astype(F32)
    return jnp.concatenate([high, x - high], axis=0).astype(BF16)


def twice(x):
    return jnp.concatenate([x, x], axis=1)


def own_lanes(pair):
    return iota((ROWS, WIDE), 0) == 2 * pair + iota((ROWS, WIDE), 1) // BLOCK


def spread(values):
    doubled = twice(values)
    return jnp.concatenate([jnp.where(own_lanes(q), doubled, 0.0) for q in range(PAIRS)], axis=1)


def fold(wide):
    kept = sum(jnp.where(own_lanes(q), wide[:, q * WIDE : (q + 1) * WIDE], 0.0) for q in range(PAIRS))
    return kept[:, :BLOCK] + kept[:, BLOCK:]


def squared(error):
    left = (iota((BLOCK, WIDE), 1) < BLOCK).astype(F32).astype(BF16)
    right = (iota((BLOCK, WIDE), 1) >= BLOCK).astype(F32).astype(BF16)
    high, low = split(error)
    weights = jnp.concatenate(
        [
            jnp.concatenate([high * left, high * right], axis=0),
            jnp.concatenate([low * left, low * right], axis=0),
        ],
        axis=1,
    )
    full = product(jnp.concatenate([high, low], axis=0), weights)
    top = full[:BLOCK] + full[BLOCK:]
    return top[:, :WIDE] + top[:, WIDE:]


def operand(errors):
    parts = [split(one) for one in errors]
    return jnp.concatenate(
        [jnp.concatenate([h for h, _ in parts], axis=1), jnp.concatenate([l for _, l in parts], axis=1)],
        axis=0,
    )


def applied(weights, values):
    full = product_nt(split_rows(spread(values)), weights)
    top = full[:ROWS] + full[ROWS:]
    return top[:, :BLOCK] + top[:, BLOCK:]


def smooth(pairs, values):
    eye = iota((BLOCK, WIDE), 0) == iota((BLOCK, WIDE), 1) % BLOCK
    sums = sum(
        jnp.where(own_lanes(q), jnp.sum(jnp.where(eye, pairs[q], 0.0), axis=0, keepdims=True), 0.0)
        for q in range(PAIRS)
    )
    inverse = 1.0 / (jnp.sum(sums, axis=1, keepdims=True) * (1.0 / BLOCK))
    one = eye.astype(F32)
    first = []
    for q in range(PAIRS):
        along = jnp.sum(jnp.where(own_lanes(q), inverse, 0.0), axis=0, keepdims=True)
        first.append(one - pairs[q] * along)
    y = values + applied(operand(first), values)
    second = [squared(e) for e in first]
    y = y + applied(operand(second), y)
    fourth = [squared(e) for e in second]
    y = y + applied(operand(fourth), y)
    y = y + applied(operand([squared(e) for e in fourth]), y)
    return y * inverse


def picked(index, values):
    return sum(jnp.where(index == x, values[x : x + 1], 0.0) for x in range(COARSE))


def restricted(index, values):
    total = jnp.zeros_like(values)
    for x in range(COARSE):
        row = jnp.sum(jnp.where(index == x, values, 0.0), axis=0, keepdims=True)
        total = total + jnp.where(iota(values.shape, 0) == x, row, 0.0)
    return total


def gathered(maps_ref, doubled):
    return [picked(maps_ref[q], doubled) for q in range(PAIRS)]


def ops_product(ops_ref, tiles):
    stacked = split_rows(jnp.concatenate(tiles, axis=1))
    full = product_nt(stacked, ops_ref[...])
    return fold(full[:ROWS] + full[ROWS:])


def fine_kernel(ops_hbm, resid_hbm, smooth_ref, rounded_ref, diag_ref, resid_ref, diag_sem, resid_sem):
    diag_copy = pltpu.make_async_copy(ops_hbm.at[:, :WIDE], diag_ref, diag_sem)
    resid_copy = pltpu.make_async_copy(resid_hbm, resid_ref, resid_sem)
    diag_copy.start()
    resid_copy.start()
    diag_copy.wait()
    resid_copy.wait()
    pairs = []
    for q in range(PAIRS):
        even = diag_ref[2 * q * BLOCK : (2 * q + 1) * BLOCK, :BLOCK].astype(F32)
        odd = diag_ref[(2 * q + 1) * BLOCK : (2 * q + 2) * BLOCK, :BLOCK].astype(F32)
        pairs.append(jnp.concatenate([even, odd], axis=1))
    out = smooth(pairs, resid_ref[...])
    smooth_ref[...] = out
    rounded_ref[...] = out.astype(BF16)


def tiles_kernel(near_ref, fine_map_ref, maps_ref, ops_ref, cols_ref, tiles_ref, acc_ref, labels_ref):
    acc_ref[...] = jnp.zeros_like(acc_ref)
    left = iota((BLOCK, WIDE), 1) < BLOCK
    unit = (iota((BLOCK, WIDE), 0) == iota((BLOCK, WIDE), 1) % BLOCK).astype(F32).astype(BF16)
    digits = [jnp.where(left, 7 * 8 ** (2 * t), 7 * 8 ** (2 * t + 1)) for t in range(LEVELS // 2)]
    rows = iota((ROWS, WIDE), 0)
    first_half = iota((ROWS, WIDE), 1) < BLOCK

    owns = []
    for j in range(FINE_BLOCKS):
        own = [fine_map_ref[j]]
        for level in range(LEVELS - 1):
            own.append(maps_ref[level, 0, own[-1]])
        word = own[0]
        for level in range(1, LEVELS):
            word = word + own[level] * 8**level
        labels_ref[j] = word
        owns.append((own, word))

    index = [jnp.where(first_half, rows, -1)] + [jnp.full((ROWS, WIDE), -1, I32) for q in range(PAIRS - 1)]
    level_cols = [jnp.zeros((ROWS, WIDE), I32) for level in range(LEVELS)]
    for j in range(FINE_BLOCKS):
        own, word = owns[j]
        others = [near_ref[j, k] for k in range(NEIGHB)]
        for level in range(LEVELS):
            level_cols[level] = jnp.where(rows == j, own[level], level_cols[level])
        for k in range(1, NEIGHB + 1):
            here = (rows == j) & (first_half if k % 2 == 0 else ~first_half)
            index[k // 2] = jnp.where(here, others[k - 1], index[k // 2])
        weights = []
        for k in range(SLOTS):
            if k > NEIGHB:
                weights.append(jnp.zeros((BLOCK, LEVELS * BLOCK), BF16))
                continue
            if k == 0:
                weights.append(jnp.concatenate([unit] * (LEVELS // 2), axis=1))
                continue
            apart = jnp.full((BLOCK, WIDE), word ^ labels_ref[others[k - 1]], I32)
            weights.append(
                jnp.concatenate(
                    [
                        unit * jnp.where((apart & digits[t]) == 0, F32(1.0), F32(0.0)).astype(BF16)
                        for t in range(LEVELS // 2)
                    ],
                    axis=1,
                )
            )
        total = product(ops_ref[j * BLOCK : (j + 1) * BLOCK, :], jnp.concatenate(weights, axis=0))
        for level in range(LEVELS):
            lanes = slice(level // 2 * WIDE, (level // 2 + 1) * WIDE)
            mine = left if level % 2 == 0 else ~left
            acc_ref[own[level], :, lanes] = acc_ref[own[level], :, lanes] + jnp.where(mine, total[:, lanes], 0.0)
    for q in range(PAIRS):
        cols_ref[q] = index[q]
    for level in range(LEVELS):
        cols_ref[PAIRS + level] = level_cols[level]
    for t in range(LEVELS // 2):
        for q in range(PAIRS):
            even, odd = (acc_ref[2 * q + i, :, t * WIDE : (t + 1) * WIDE] for i in range(2))
            tiles_ref[2 * t, q] = jnp.where(left, even, pltpu.roll(odd, BLOCK, 1))
            tiles_ref[2 * t + 1, q] = jnp.where(left, pltpu.roll(even, BLOCK, 1), odd)


HEAD = 2 * ROWS
HALF = BLOCK // 2
SEND0 = HEAD + PAIRS * BLOCK + 2 * BLOCK
SEND1 = HEAD + 2 * BLOCK + BLOCK
SEND2 = HEAD + BLOCK + HALF
SEND3 = HEAD + HALF


def on_diagonal(size, start):
    return iota((size, WIDE), 0) + start == iota((size, WIDE), 1) % BLOCK


def packed(values, parts):
    head = jnp.concatenate([values.astype(BF16).astype(F32), values - values.astype(BF16).astype(F32)], axis=1)
    rows = iota((ROWS, WIDE), 0)
    lows = jnp.zeros((ROWS, WIDE), F32)
    body = []
    for i, (part, start) in enumerate(parts):
        high, low = split(part)
        body.append(high)
        along = jnp.where(on_diagonal(part.shape[0], start), low.astype(F32), 0.0)
        lows = jnp.where(rows == i, jnp.sum(along, axis=0, keepdims=True), lows)
    return jnp.concatenate([jnp.concatenate([head, lows], axis=0).astype(BF16)] + body, axis=0)


def got_rows(ref, base):
    head = ref[base : base + HEAD, :].astype(F32)[:ROWS]
    return head[:, :BLOCK] + head[:, BLOCK:]


def got_part(ref, base, i, at, size, start):
    low = ref[base : base + HEAD, :].astype(F32)[ROWS + i : ROWS + i + 1]
    high = ref[base + at : base + at + size, :].astype(F32)
    return high + jnp.where(on_diagonal(size, start), low, 0.0)


def resid_kernel(ops_ref, resid_ref, rounded_ref, earlier_ref, cols_ref, tiles_ref, fresid_ref, rows_ref, send_ref):
    own = twice(rounded_ref[...].astype(F32))
    before = twice(earlier_ref[...].astype(F32))
    tiles = gathered(cols_ref, own)
    tiles[-1] = jnp.where(iota((ROWS, WIDE), 1) < BLOCK, tiles[-1], before)
    stacked = jnp.concatenate(tiles, axis=1)
    stacked = jnp.concatenate([stacked, jnp.zeros_like(stacked)], axis=0).astype(BF16)
    fresid = resid_ref[...] - fold(product_nt(stacked, ops_ref[...])[:ROWS])
    fresid_ref[...] = fresid
    rows = restricted(cols_ref[PAIRS][:, :BLOCK], fresid)
    rows_ref[...] = rows
    other = 1 - lax.rem(lax.axis_index("gy"), 2)
    parts = [(tiles_ref[0, q], 0) for q in range(PAIRS)] + [(tiles_ref[1, 2 * other + i], 0) for i in range(2)]
    send_ref[...] = packed(rows, parts)


def descend(level, pairs, coarse_rows, ops_ref, cols_ref, fresid_ref, total_ref, fresid_out, total_out):
    out = smooth(pairs, coarse_rows)
    on_fine = picked(cols_ref[PAIRS + level][:, :BLOCK], out)
    total_out[...] = total_ref[...] + on_fine
    fresid = fresid_ref[...] - ops_product(ops_ref, gathered(cols_ref, twice(on_fine)))
    if fresid_out is not None:
        fresid_out[...] = fresid
    return restricted(cols_ref[PAIRS + level + 1][:, :BLOCK], fresid)


def level0_kernel(ops_ref, cols_ref, tiles_ref, rows_ref, got_ref, fresid_ref, total_ref, fresid_out, total_out, send_ref):
    half = lax.rem(lax.axis_index("gy"), 2)
    received = [got_part(got_ref, 0, i, HEAD + i * BLOCK, BLOCK, 0) for i in range(PAIRS + 2)]
    pairs = [tiles_ref[0, q] + received[q] for q in range(PAIRS)]
    coarse_rows = rows_ref[...] + got_rows(got_ref, 0)
    summed = [tiles_ref[1, 2 * half + i] + received[PAIRS + i] for i in range(2)]
    rows = descend(0, pairs, coarse_rows, ops_ref, cols_ref, fresid_ref, total_ref, fresid_out, total_out)
    for e in range(4):
        parts = [(summed[0], 0), (summed[1], 0), (tiles_ref[2, e], 0)]
        send_ref[e * SEND1 : (e + 1) * SEND1, :] = packed(rows, parts)


def level1_kernel(ops_ref, cols_ref, tiles_ref, got_ref, fresid_ref, total_ref, fresid_out, total_out, send_ref):
    coarse_rows = sum(got_rows(got_ref, e * SEND1) for e in range(4))
    pairs = []
    for q in range(PAIRS):
        half, i = q // 2, q % 2
        pairs.append(
            sum(got_part(got_ref, e * SEND1, i, HEAD + i * BLOCK, BLOCK, 0) for e in (half, half + 2))
        )
    summed = sum(got_part(got_ref, e * SEND1, 2, HEAD + 2 * BLOCK, BLOCK, 0) for e in range(4))
    rows = descend(1, pairs, coarse_rows, ops_ref, cols_ref, fresid_ref, total_ref, fresid_out, total_out)
    for e in range(8):
        start = HALF * (e % 2)
        parts = [(summed, 0), (tiles_ref[3, e // 2, start : start + HALF, :], start)]
        send_ref[e * SEND2 : (e + 1) * SEND2, :] = packed(rows, parts)


def level2_kernel(ops_ref, cols_ref, got_ref, fresid_ref, total_ref, total_out, rows_out, part_out, send_ref):
    coarse_rows = sum(got_rows(got_ref, e * SEND2) for e in range(8))
    pairs = [
        sum(got_part(got_ref, e * SEND2, 0, HEAD, BLOCK, 0) for e in (q, q + 4)) for q in range(PAIRS)
    ]
    start = HALF * lax.rem(lax.axis_index("gy"), 2)
    summed = sum(got_part(got_ref, e * SEND2, 1, HEAD + BLOCK, HALF, start) for e in range(8))
    rows = descend(2, pairs, coarse_rows, ops_ref, cols_ref, fresid_ref, total_ref, None, total_out)
    rows_out[...] = rows
    part_out[...] = summed
    send_ref[...] = packed(rows, [(summed, start)])


def join_kernel(rows_ref, part_ref, got_ref, send_ref):
    start = HALF * lax.rem(lax.axis_index("gy"), 2)
    rows = rows_ref[...] + got_rows(got_ref, 0)
    chunk = packed(rows, [(part_ref[...] + got_part(got_ref, 0, 0, HEAD, HALF, start), start)])
    for e in range(8):
        send_ref[e * SEND3 : (e + 1) * SEND3, :] = chunk


def level3_kernel(cols_ref, got_ref, total_ref, out_ref):
    coarse_rows = sum(got_rows(got_ref, e * SEND3) for e in range(8))
    eighths = [got_part(got_ref, e * SEND3, 0, HEAD, HALF, HALF * (e % 2)) for e in range(8)]
    pairs = [jnp.concatenate([eighths[2 * q], eighths[2 * q + 1]], axis=0) for q in range(PAIRS)]
    out = smooth(pairs, coarse_rows)
    out_ref[...] = total_ref[...] + picked(cols_ref[PAIRS + 3][:, :BLOCK], out)


def call(kernel, name, out_shapes, args, scalars=0, scratch=(), outside=0, grant=GRANT):
    hbm = pl.BlockSpec(memory_space=pltpu.HBM)
    vmem = pl.BlockSpec(memory_space=pltpu.VMEM)
    smem = pl.BlockSpec(memory_space=pltpu.SMEM)
    return pl.pallas_call(
        kernel,
        name=name,
        out_shape=[jax.ShapeDtypeStruct(shape, kind) for shape, kind in out_shapes],
        in_specs=[smem] * scalars + [hbm] * outside + [vmem] * (len(args) - scalars - outside),
        out_specs=[vmem] * len(out_shapes),
        scratch_shapes=list(scratch),
        compiler_params=pltpu.CompilerParams(vmem_limit_bytes=grant),
        interpret=INTERPRET,
    )(*args)


def shared(chunks, size):
    lists = [[g * size + i for i in range(size)] for g in range(lax.axis_size("gy") // size)]
    return lax.all_to_all(chunks, "gy", 0, 0, axis_index_groups=lists, tiled=True)


def crossed(value, distance):
    return lax.ppermute(value, "gy", [(i, i ^ distance) for i in range(lax.axis_size("gy"))])


def on_device(residual, fine_ops, neighbours, fine_map, coarse_maps):
    ops = fine_ops.reshape(FINE_BLOCKS * BLOCK, SLOTS * BLOCK)
    vec = (FINE_BLOCKS, BLOCK)
    fine_smooth, rounded = call(
        fine_kernel,
        "fine_smooth",
        [(vec, F32), (vec, BF16)],
        [ops, residual],
        outside=2,
        grant=FIRST_GRANT,
        scratch=[
            pltpu.VMEM((FINE_BLOCKS * BLOCK, WIDE), BF16),
            pltpu.VMEM(vec, F32),
            pltpu.SemaphoreType.DMA,
            pltpu.SemaphoreType.DMA,
        ],
    )
    earlier = lax.ppermute(rounded, "ta", [(0, 1)])
    cols, tiles = call(
        tiles_kernel,
        "tile_parts",
        [((PAIRS + LEVELS, ROWS, WIDE), I32), ((LEVELS, PAIRS, BLOCK, WIDE), F32)],
        [neighbours, fine_map, jnp.transpose(coarse_maps, (1, 0, 2)), ops],
        scalars=3,
        scratch=[pltpu.VMEM((COARSE, BLOCK, LEVELS * BLOCK), F32), pltpu.SMEM((FINE_BLOCKS,), I32)],
    )
    fresid, rows, sent = call(
        resid_kernel,
        "fine_resid",
        [(vec, F32), (vec, F32), ((SEND0, WIDE), BF16)],
        [ops, residual, rounded, earlier, cols, tiles],
    )
    got = crossed(sent, 1)
    fresid, total, chunks = call(
        level0_kernel,
        "level_0",
        [(vec, F32), (vec, F32), ((4 * SEND1, WIDE), BF16)],
        [ops, cols, tiles, rows, got, fresid, fine_smooth],
    )
    got = shared(chunks, 4)
    fresid, total, chunks = call(
        level1_kernel,
        "level_1",
        [(vec, F32), (vec, F32), ((8 * SEND2, WIDE), BF16)],
        [ops, cols, tiles, got, fresid, total],
    )
    got = shared(chunks, 8)
    total, rows, part, sent = call(
        level2_kernel,
        "level_2",
        [(vec, F32), (vec, F32), ((HALF, WIDE), F32), ((SEND3, WIDE), BF16)],
        [ops, cols, got, fresid, total],
    )
    got = crossed(sent, 8)
    (chunks,) = call(join_kernel, "join", [((8 * SEND3, WIDE), BF16)], [rows, part, got])
    got = shared(chunks, 8)
    (out,) = call(level3_kernel, "level_3", [(vec, F32)], [cols, got, total])
    return out


def solution(mesh):
    return jax.shard_map(
        on_device,
        mesh=mesh,
        in_specs=(
            P(("gx", "gy", "ta"), None),
            P(("gx", "gy", "ta"), None, None),
            P(("gx", "gy", "ta"), None),
            P(("gx", "gy", "ta")),
            P(("gx", "gy", "ta"), None, None),
        ),
        out_specs=P(("gx", "gy", "ta"), None),
        check_vma=False,
    )
```

```python
import jax
import jax.numpy as jnp
from jax import lax
from jax.experimental import pallas as pl
from jax.experimental.pallas import tpu as pltpu
from jax.sharding import PartitionSpec as P

BLOCK = 64
SLOTS = 8
NEIGHB = 6
COARSE = 8
LEVELS = 4
FINE_BLOCKS = 8
PAIRS = COARSE // 2
WIDE = 2 * BLOCK
ROWS = COARSE
GRANT = 12 * 2**20
INTERPRET = False

F32 = jnp.float32
BF16 = jnp.bfloat16
I32 = jnp.int32


def iota(shape, axis):
    return lax.broadcasted_iota(I32, shape, axis)


def product(x, weights):
    return jnp.dot(x, weights, preferred_element_type=F32)


def product_nt(x, weights):
    return lax.dot_general(x, weights, (((1,), (1,)), ((), ())), preferred_element_type=F32)


def split(x):
    high = x.astype(BF16)
    return high, (x - high.astype(F32)).astype(BF16)


def split_rows(x):
    high = x.astype(BF16).astype(F32)
    return jnp.concatenate([high, x - high], axis=0).astype(BF16)


def twice(x):
    return jnp.concatenate([x, x], axis=1)


def own_lanes(pair):
    return iota((ROWS, WIDE), 0) == 2 * pair + iota((ROWS, WIDE), 1) // BLOCK


def spread(values):
    return jnp.concatenate([jnp.where(own_lanes(q), values, 0.0) for q in range(PAIRS)], axis=1)


def fold(wide):
    kept = sum(jnp.where(own_lanes(q), wide[:, q * WIDE : (q + 1) * WIDE], 0.0) for q in range(PAIRS))
    return kept + pltpu.roll(kept, BLOCK, 1)


def squared(error):
    left = (iota((BLOCK, WIDE), 1) < BLOCK).astype(F32).astype(BF16)
    right = (iota((BLOCK, WIDE), 1) >= BLOCK).astype(F32).astype(BF16)
    high, low = split(error)
    weights = jnp.concatenate(
        [
            jnp.concatenate([high * left, high * right], axis=0),
            jnp.concatenate([low * left, low * right], axis=0),
        ],
        axis=1,
    )
    full = product(jnp.concatenate([high, low], axis=0), weights)
    top = full[:BLOCK] + full[BLOCK:]
    return top[:, :WIDE] + top[:, WIDE:]


def operand(errors):
    parts = [split(one) for one in errors]
    return jnp.concatenate(
        [jnp.concatenate([h for h, _ in parts], axis=1), jnp.concatenate([l for _, l in parts], axis=1)],
        axis=0,
    )


def applied(weights, values):
    full = product_nt(split_rows(spread(values)), weights)
    top = full[:ROWS] + full[ROWS:]
    return top + pltpu.roll(top, BLOCK, 1)


def smooth_steps(pairs, values):
    eye = iota((BLOCK, WIDE), 0) == iota((BLOCK, WIDE), 1) % BLOCK
    sums = sum(
        jnp.where(own_lanes(q), jnp.sum(jnp.where(eye, pairs[q], 0.0), axis=0, keepdims=True), 0.0)
        for q in range(PAIRS)
    )
    inverse = 1.0 / (jnp.sum(sums, axis=1, keepdims=True) * (1.0 / BLOCK))
    one = eye.astype(F32)
    first = []
    for q in range(PAIRS):
        along = jnp.sum(jnp.where(own_lanes(q), inverse, 0.0), axis=0, keepdims=True)
        first.append(one - pairs[q] * along)
    y = values + applied(operand(first), values)
    second = [squared(e) for e in first]
    yield None
    y = y + applied(operand(second), y)
    fourth = [squared(e) for e in second]
    yield None
    y = y + applied(operand(fourth), y)
    eighth = [squared(e) for e in fourth]
    yield None
    y = y + applied(operand(eighth), y)
    yield y * inverse


def smooth(pairs, values):
    return list(smooth_steps(pairs, values))[-1]


def picked(index, values):
    return sum(jnp.where(index == x, values[x : x + 1], 0.0) for x in range(COARSE))


def restricted(index, values):
    total = jnp.zeros_like(values)
    for x in range(COARSE):
        row = jnp.sum(jnp.where(index == x, values, 0.0), axis=0, keepdims=True)
        total = total + jnp.where(iota(values.shape, 0) == x, row, 0.0)
    return total


def gathered(maps_ref, doubled):
    return [picked(maps_ref[q], doubled) for q in range(PAIRS)]


def ops_product(ops_ref, tiles):
    stacked = split_rows(jnp.concatenate(tiles, axis=1))
    full = product_nt(stacked, ops_ref[...])
    return fold(full[:ROWS] + full[ROWS:])


def first_kernel(*refs):
    sources, refs = refs[:5], refs[5:]
    (smooth_ref, rounded_ref, cols_ref, tiles_ref), refs = refs[:4], refs[4:]
    held, (acc_ref, labels_ref, sems) = refs[:5], refs[5:]
    copies = [pltpu.make_async_copy(sources[i], held[i], sems.at[i]) for i in range(5)]
    for copy in copies:
        copy.start()
    near_ref, fine_map_ref, maps_ref, ops_ref, resid_ref = held
    acc_ref[...] = jnp.zeros_like(acc_ref)
    for copy in copies[:3]:
        copy.wait()
    left = iota((BLOCK, WIDE), 1) < BLOCK
    unit = (iota((BLOCK, WIDE), 0) == iota((BLOCK, WIDE), 1) % BLOCK).astype(F32).astype(BF16)
    digits = [jnp.where(left, 7 * 8 ** (2 * t), 7 * 8 ** (2 * t + 1)) for t in range(LEVELS // 2)]
    rows = iota((ROWS, WIDE), 0)
    first_half = iota((ROWS, WIDE), 1) < BLOCK

    owns = []
    for j in range(FINE_BLOCKS):
        own = [fine_map_ref[j]]
        for level in range(LEVELS - 1):
            own.append(maps_ref[level, 0, own[-1]])
        word = own[0]
        for level in range(1, LEVELS):
            word = word + own[level] * 8**level
        labels_ref[j] = word
        owns.append((own, word))

    for copy in copies[3:]:
        copy.wait()
    pairs = []
    for q in range(PAIRS):
        even = ops_ref[2 * q * BLOCK : (2 * q + 1) * BLOCK, :BLOCK].astype(F32)
        odd = ops_ref[(2 * q + 1) * BLOCK : (2 * q + 2) * BLOCK, :BLOCK].astype(F32)
        pairs.append(jnp.concatenate([even, odd], axis=1))
    steps = smooth_steps(pairs, twice(resid_ref[...]))
    index = [jnp.where(first_half, rows, -1)] + [jnp.full((ROWS, WIDE), -1, I32) for q in range(PAIRS - 1)]
    level_cols = [jnp.zeros((ROWS, WIDE), I32) for level in range(LEVELS)]
    for j in range(FINE_BLOCKS):
        own, word = owns[j]
        others = [near_ref[j, k] for k in range(NEIGHB)]
        for level in range(LEVELS):
            level_cols[level] = jnp.where(rows == j, own[level], level_cols[level])
        for k in range(1, NEIGHB + 1):
            here = (rows == j) & (first_half if k % 2 == 0 else ~first_half)
            index[k // 2] = jnp.where(here, others[k - 1], index[k // 2])
        weights = []
        for k in range(SLOTS):
            if k > NEIGHB:
                weights.append(jnp.zeros((BLOCK, LEVELS * BLOCK), BF16))
                continue
            if k == 0:
                weights.append(jnp.concatenate([unit] * (LEVELS // 2), axis=1))
                continue
            apart = jnp.full((BLOCK, WIDE), word ^ labels_ref[others[k - 1]], I32)
            weights.append(
                jnp.concatenate(
                    [
                        unit * jnp.where((apart & digits[t]) == 0, F32(1.0), F32(0.0)).astype(BF16)
                        for t in range(LEVELS // 2)
                    ],
                    axis=1,
                )
            )
        total = product(ops_ref[j * BLOCK : (j + 1) * BLOCK, :], jnp.concatenate(weights, axis=0))
        for level in range(LEVELS):
            lanes = slice(level // 2 * WIDE, (level // 2 + 1) * WIDE)
            mine = left if level % 2 == 0 else ~left
            acc_ref[own[level], :, lanes] = acc_ref[own[level], :, lanes] + jnp.where(mine, total[:, lanes], 0.0)
        if j % 2 == 1:
            out = next(steps)
    smooth_ref[...] = out
    rounded_ref[...] = out.astype(BF16)
    for q in range(PAIRS):
        cols_ref[q] = index[q]
    for level in range(LEVELS):
        cols_ref[PAIRS + level] = level_cols[level]
    for t in range(LEVELS // 2):
        for q in range(PAIRS):
            even, odd = (acc_ref[2 * q + i, :, t * WIDE : (t + 1) * WIDE] for i in range(2))
            tiles_ref[2 * t, q] = jnp.where(left, even, pltpu.roll(odd, BLOCK, 1))
            tiles_ref[2 * t + 1, q] = jnp.where(left, pltpu.roll(even, BLOCK, 1), odd)


HEAD = 2 * ROWS
HALF = BLOCK // 2
SEND0 = HEAD + PAIRS * BLOCK + 2 * BLOCK
SEND1 = HEAD + 2 * BLOCK + BLOCK
SEND2 = HEAD + BLOCK + HALF
SEND3 = HEAD + HALF


def on_diagonal(size, start):
    return iota((size, WIDE), 0) + start == iota((size, WIDE), 1) % BLOCK


def packed(values, parts):
    rows = iota((ROWS, WIDE), 0)
    near = values.astype(BF16).astype(F32)
    head = jnp.where(iota((ROWS, WIDE), 1) < BLOCK, near, values - near)
    lows = jnp.zeros((ROWS, WIDE), F32)
    body = []
    for i, (part, start) in enumerate(parts):
        high, low = split(part)
        body.append(high)
        along = jnp.where(on_diagonal(part.shape[0], start), low.astype(F32), 0.0)
        lows = jnp.where(rows == i, jnp.sum(along, axis=0, keepdims=True), lows)
    return jnp.concatenate([jnp.concatenate([head, lows], axis=0).astype(BF16)] + body, axis=0)


def got_rows(ref, base):
    head = ref[base : base + HEAD, :].astype(F32)[:ROWS]
    return head + pltpu.roll(head, BLOCK, 1)


def got_part(ref, base, i, at, size, start):
    low = ref[base : base + HEAD, :].astype(F32)[ROWS + i : ROWS + i + 1]
    high = ref[base + at : base + at + size, :].astype(F32)
    return high + jnp.where(on_diagonal(size, start), low, 0.0)


def resid_kernel(ops_ref, resid_ref, rounded_ref, earlier_ref, cols_ref, tiles_ref, fresid_ref, rows_ref, send_ref):
    own = rounded_ref[...].astype(F32)
    before = earlier_ref[...].astype(F32)
    tiles = gathered(cols_ref, own)
    tiles[-1] = jnp.where(iota((ROWS, WIDE), 1) < BLOCK, tiles[-1], before)
    stacked = jnp.concatenate(tiles, axis=1)
    stacked = jnp.concatenate([stacked, jnp.zeros_like(stacked)], axis=0).astype(BF16)
    fresid = twice(resid_ref[...]) - fold(product_nt(stacked, ops_ref[...])[:ROWS])
    fresid_ref[...] = fresid
    rows = restricted(cols_ref[PAIRS], fresid)
    rows_ref[...] = rows
    other = 1 - lax.rem(lax.axis_index("gy"), 2)
    parts = [(tiles_ref[0, q], 0) for q in range(PAIRS)] + [(tiles_ref[1, 2 * other + i], 0) for i in range(2)]
    send_ref[...] = packed(rows, parts)


def descend(level, pairs, coarse_rows, ops_ref, cols_ref, fresid_ref, total_ref, fresid_out, total_out):
    out = smooth(pairs, coarse_rows)
    on_fine = picked(cols_ref[PAIRS + level], out)
    total_out[...] = total_ref[...] + on_fine
    fresid = fresid_ref[...] - ops_product(ops_ref, gathered(cols_ref, on_fine))
    if fresid_out is not None:
        fresid_out[...] = fresid
    return restricted(cols_ref[PAIRS + level + 1], fresid)


def level0_kernel(ops_ref, cols_ref, tiles_ref, rows_ref, got_ref, fresid_ref, total_ref, fresid_out, total_out, send_ref):
    half = lax.rem(lax.axis_index("gy"), 2)
    received = [got_part(got_ref, 0, i, HEAD + i * BLOCK, BLOCK, 0) for i in range(PAIRS + 2)]
    pairs = [tiles_ref[0, q] + received[q] for q in range(PAIRS)]
    coarse_rows = rows_ref[...] + got_rows(got_ref, 0)
    summed = [tiles_ref[1, 2 * half + i] + received[PAIRS + i] for i in range(2)]
    rows = descend(0, pairs, coarse_rows, ops_ref, cols_ref, fresid_ref, total_ref, fresid_out, total_out)
    for e in range(4):
        parts = [(summed[0], 0), (summed[1], 0), (tiles_ref[2, e], 0)]
        send_ref[e * SEND1 : (e + 1) * SEND1, :] = packed(rows, parts)


def level1_kernel(ops_ref, cols_ref, tiles_ref, got_ref, fresid_ref, total_ref, fresid_out, total_out, send_ref):
    coarse_rows = sum(got_rows(got_ref, e * SEND1) for e in range(4))
    pairs = []
    for q in range(PAIRS):
        half, i = q // 2, q % 2
        pairs.append(
            sum(got_part(got_ref, e * SEND1, i, HEAD + i * BLOCK, BLOCK, 0) for e in (half, half + 2))
        )
    summed = sum(got_part(got_ref, e * SEND1, 2, HEAD + 2 * BLOCK, BLOCK, 0) for e in range(4))
    rows = descend(1, pairs, coarse_rows, ops_ref, cols_ref, fresid_ref, total_ref, fresid_out, total_out)
    for e in range(8):
        start = HALF * (e % 2)
        parts = [(summed, 0), (tiles_ref[3, e // 2, start : start + HALF, :], start)]
        send_ref[e * SEND2 : (e + 1) * SEND2, :] = packed(rows, parts)


def level2_kernel(ops_ref, cols_ref, got_ref, fresid_ref, total_ref, total_out, rows_out, part_out, send_ref):
    coarse_rows = sum(got_rows(got_ref, e * SEND2) for e in range(8))
    pairs = [
        sum(got_part(got_ref, e * SEND2, 0, HEAD, BLOCK, 0) for e in (q, q + 4)) for q in range(PAIRS)
    ]
    start = HALF * lax.rem(lax.axis_index("gy"), 2)
    summed = sum(got_part(got_ref, e * SEND2, 1, HEAD + BLOCK, HALF, start) for e in range(8))
    rows = descend(2, pairs, coarse_rows, ops_ref, cols_ref, fresid_ref, total_ref, None, total_out)
    rows_out[...] = rows
    part_out[...] = summed
    send_ref[...] = packed(rows, [(summed, start)])


def join_kernel(rows_ref, part_ref, got_ref, send_ref):
    start = HALF * lax.rem(lax.axis_index("gy"), 2)
    rows = rows_ref[...] + got_rows(got_ref, 0)
    chunk = packed(rows, [(part_ref[...] + got_part(got_ref, 0, 0, HEAD, HALF, start), start)])
    for e in range(8):
        send_ref[e * SEND3 : (e + 1) * SEND3, :] = chunk


def level3_kernel(cols_ref, got_ref, total_ref, out_ref):
    coarse_rows = sum(got_rows(got_ref, e * SEND3) for e in range(8))
    eighths = [got_part(got_ref, e * SEND3, 0, HEAD, HALF, HALF * (e % 2)) for e in range(8)]
    pairs = [jnp.concatenate([eighths[2 * q], eighths[2 * q + 1]], axis=0) for q in range(PAIRS)]
    out = smooth(pairs, coarse_rows)
    out_ref[...] = (total_ref[...] + picked(cols_ref[PAIRS + 3], out))[:, :BLOCK]


def call(kernel, name, out_shapes, args, scratch=(), outside=0):
    hbm = pl.BlockSpec(memory_space=pltpu.HBM)
    vmem = pl.BlockSpec(memory_space=pltpu.VMEM)
    return pl.pallas_call(
        kernel,
        name=name,
        out_shape=[jax.ShapeDtypeStruct(shape, kind) for shape, kind in out_shapes],
        in_specs=[hbm] * outside + [vmem] * (len(args) - outside),
        out_specs=[vmem] * len(out_shapes),
        scratch_shapes=list(scratch),
        compiler_params=pltpu.CompilerParams(vmem_limit_bytes=GRANT),
        interpret=INTERPRET,
    )(*args)


def shared(chunks, size):
    lists = [[g * size + i for i in range(size)] for g in range(lax.axis_size("gy") // size)]
    return lax.all_to_all(chunks, "gy", 0, 0, axis_index_groups=lists, tiled=True)


def crossed(value, distance):
    return lax.ppermute(value, "gy", [(i, i ^ distance) for i in range(lax.axis_size("gy"))])


def on_device(residual, fine_ops, neighbours, fine_map, coarse_maps):
    ops = fine_ops.reshape(FINE_BLOCKS * BLOCK, SLOTS * BLOCK)
    vec = (FINE_BLOCKS, WIDE)
    fine_smooth, rounded, cols, tiles = call(
        first_kernel,
        "first",
        [(vec, F32), (vec, BF16), ((PAIRS + LEVELS, ROWS, WIDE), I32), ((LEVELS, PAIRS, BLOCK, WIDE), F32)],
        [
            pltpu.with_memory_space_constraint(x, pltpu.HBM)
            for x in (neighbours, fine_map, jnp.transpose(coarse_maps, (1, 0, 2)), ops, residual)
        ],
        outside=5,
        scratch=[
            pltpu.SMEM((FINE_BLOCKS, NEIGHB), I32),
            pltpu.SMEM((FINE_BLOCKS,), I32),
            pltpu.SMEM((LEVELS - 1, 1, COARSE), I32),
            pltpu.VMEM((FINE_BLOCKS * BLOCK, SLOTS * BLOCK), BF16),
            pltpu.VMEM((FINE_BLOCKS, BLOCK), F32),
            pltpu.VMEM((COARSE, BLOCK, LEVELS * BLOCK), F32),
            pltpu.SMEM((FINE_BLOCKS,), I32),
            pltpu.SemaphoreType.DMA((5,)),
        ],
    )
    earlier = lax.ppermute(rounded, "ta", [(0, 1)])
    fresid, rows, sent = call(
        resid_kernel,
        "fine_resid",
        [(vec, F32), (vec, F32), ((SEND0, WIDE), BF16)],
        [ops, residual, rounded, earlier, cols, tiles],
    )
    got = crossed(sent, 1)
    fresid, total, chunks = call(
        level0_kernel,
        "level_0",
        [(vec, F32), (vec, F32), ((4 * SEND1, WIDE), BF16)],
        [ops, cols, tiles, rows, got, fresid, fine_smooth],
    )
    got = shared(chunks, 4)
    fresid, total, chunks = call(
        level1_kernel,
        "level_1",
        [(vec, F32), (vec, F32), ((8 * SEND2, WIDE), BF16)],
        [ops, cols, tiles, got, fresid, total],
    )
    got = shared(chunks, 8)
    total, rows, part, sent = call(
        level2_kernel,
        "level_2",
        [(vec, F32), (vec, F32), ((HALF, WIDE), F32), ((SEND3, WIDE), BF16)],
        [ops, cols, got, fresid, total],
    )
    got = crossed(sent, 8)
    (chunks,) = call(join_kernel, "join", [((8 * SEND3, WIDE), BF16)], [rows, part, got])
    got = shared(chunks, 8)
    (out,) = call(level3_kernel, "level_3", [((FINE_BLOCKS, BLOCK), F32)], [cols, got, total])
    return out


def solution(mesh):
    return jax.shard_map(
        on_device,
        mesh=mesh,
        in_specs=(
            P(("gx", "gy", "ta"), None),
            P(("gx", "gy", "ta"), None, None),
            P(("gx", "gy", "ta"), None),
            P(("gx", "gy", "ta")),
            P(("gx", "gy", "ta"), None, None),
        ),
        out_specs=P(("gx", "gy", "ta"), None),
        check_vma=False,
    )
```

```python
import jax
import jax.numpy as jnp
from jax import lax
from jax.experimental import pallas as pl
from jax.experimental.pallas import tpu as pltpu
from jax.sharding import PartitionSpec as P

BLOCK = 64
SLOTS = 8
NEIGHB = 6
COARSE = 8
LEVELS = 4
FINE_BLOCKS = 8
PAIRS = COARSE // 2
WIDE = 2 * BLOCK
ROWS = COARSE
GRANT = 12 * 2**20
INTERPRET = False

F32 = jnp.float32
BF16 = jnp.bfloat16
I32 = jnp.int32


def iota(shape, axis):
    return lax.broadcasted_iota(I32, shape, axis)


def product(x, weights):
    return jnp.dot(x, weights, preferred_element_type=F32)


def product_nt(x, weights):
    return lax.dot_general(x, weights, (((1,), (1,)), ((), ())), preferred_element_type=F32)


def split(x):
    high = x.astype(BF16)
    return high, (x - high.astype(F32)).astype(BF16)


def split_rows(x):
    high = x.astype(BF16).astype(F32)
    return jnp.concatenate([high, x - high], axis=0).astype(BF16)


def twice(x):
    return jnp.concatenate([x, x], axis=1)


def own_lanes(pair):
    return iota((ROWS, WIDE), 0) == 2 * pair + iota((ROWS, WIDE), 1) // BLOCK


def spread(values):
    return jnp.concatenate([jnp.where(own_lanes(q), values, 0.0) for q in range(PAIRS)], axis=1)


def fold(wide):
    kept = sum(jnp.where(own_lanes(q), wide[:, q * WIDE : (q + 1) * WIDE], 0.0) for q in range(PAIRS))
    return kept + pltpu.roll(kept, BLOCK, 1)


def squared(error):
    left = (iota((BLOCK, WIDE), 1) < BLOCK).astype(F32).astype(BF16)
    right = (iota((BLOCK, WIDE), 1) >= BLOCK).astype(F32).astype(BF16)
    high, low = split(error)
    weights = jnp.concatenate(
        [
            jnp.concatenate([high * left, high * right], axis=0),
            jnp.concatenate([low * left, low * right], axis=0),
        ],
        axis=1,
    )
    full = product(jnp.concatenate([high, low], axis=0), weights)
    top = full[:BLOCK] + full[BLOCK:]
    return top[:, :WIDE] + top[:, WIDE:]


def operand(errors):
    parts = [split(one) for one in errors]
    return jnp.concatenate(
        [jnp.concatenate([h for h, _ in parts], axis=1), jnp.concatenate([l for _, l in parts], axis=1)],
        axis=0,
    )


def applied(weights, values):
    full = product_nt(split_rows(spread(values)), weights)
    top = full[:ROWS] + full[ROWS:]
    return top + pltpu.roll(top, BLOCK, 1)


def smooth(pairs, values):
    eye = iota((BLOCK, WIDE), 0) == iota((BLOCK, WIDE), 1) % BLOCK
    sums = sum(
        jnp.where(own_lanes(q), jnp.sum(jnp.where(eye, pairs[q], 0.0), axis=0, keepdims=True), 0.0)
        for q in range(PAIRS)
    )
    inverse = 1.0 / (jnp.sum(sums, axis=1, keepdims=True) * (1.0 / BLOCK))
    one = eye.astype(F32)
    first = []
    for q in range(PAIRS):
        along = jnp.sum(jnp.where(own_lanes(q), inverse, 0.0), axis=0, keepdims=True)
        first.append(one - pairs[q] * along)
    y = values + applied(operand(first), values)
    second = [squared(e) for e in first]
    y = y + applied(operand(second), y)
    fourth = [squared(e) for e in second]
    y = y + applied(operand(fourth), y)
    y = y + applied(operand([squared(e) for e in fourth]), y)
    return y * inverse


def picked(index, values):
    return sum(jnp.where(index == x, values[x : x + 1], 0.0) for x in range(COARSE))


def restricted(index, values):
    total = jnp.zeros_like(values)
    for x in range(COARSE):
        row = jnp.sum(jnp.where(index == x, values, 0.0), axis=0, keepdims=True)
        total = total + jnp.where(iota(values.shape, 0) == x, row, 0.0)
    return total


def gathered(maps_ref, doubled):
    return [picked(maps_ref[q], doubled) for q in range(PAIRS)]


def ops_product(ops_ref, tiles):
    stacked = split_rows(jnp.concatenate(tiles, axis=1))
    full = product_nt(stacked, ops_ref[...])
    return fold(full[:ROWS] + full[ROWS:])


def fine_kernel(ops_hbm, resid_hbm, smooth_ref, rounded_ref, diag_ref, resid_ref, diag_sem, resid_sem):
    diag_copy = pltpu.make_async_copy(ops_hbm.at[:, :WIDE], diag_ref, diag_sem)
    resid_copy = pltpu.make_async_copy(resid_hbm, resid_ref, resid_sem)
    diag_copy.start()
    resid_copy.start()
    diag_copy.wait()
    resid_copy.wait()
    pairs = []
    for q in range(PAIRS):
        even = diag_ref[2 * q * BLOCK : (2 * q + 1) * BLOCK, :BLOCK].astype(F32)
        odd = diag_ref[(2 * q + 1) * BLOCK : (2 * q + 2) * BLOCK, :BLOCK].astype(F32)
        pairs.append(jnp.concatenate([even, odd], axis=1))
    out = smooth(pairs, twice(resid_ref[...]))
    smooth_ref[...] = out
    rounded_ref[...] = out.astype(BF16)


def tiles_kernel(near_ref, fine_map_ref, maps_ref, ops_ref, cols_ref, tiles_ref, acc_ref, labels_ref):
    acc_ref[...] = jnp.zeros_like(acc_ref)
    left = iota((BLOCK, WIDE), 1) < BLOCK
    unit = (iota((BLOCK, WIDE), 0) == iota((BLOCK, WIDE), 1) % BLOCK).astype(F32).astype(BF16)
    digits = [jnp.where(left, 7 * 8 ** (2 * t), 7 * 8 ** (2 * t + 1)) for t in range(LEVELS // 2)]
    rows = iota((ROWS, WIDE), 0)
    first_half = iota((ROWS, WIDE), 1) < BLOCK

    owns = []
    for j in range(FINE_BLOCKS):
        own = [fine_map_ref[j]]
        for level in range(LEVELS - 1):
            own.append(maps_ref[level, 0, own[-1]])
        word = own[0]
        for level in range(1, LEVELS):
            word = word + own[level] * 8**level
        labels_ref[j] = word
        owns.append((own, word))

    index = [jnp.where(first_half, rows, -1)] + [jnp.full((ROWS, WIDE), -1, I32) for q in range(PAIRS - 1)]
    level_cols = [jnp.zeros((ROWS, WIDE), I32) for level in range(LEVELS)]
    for j in range(FINE_BLOCKS):
        own, word = owns[j]
        others = [near_ref[j, k] for k in range(NEIGHB)]
        for level in range(LEVELS):
            level_cols[level] = jnp.where(rows == j, own[level], level_cols[level])
        for k in range(1, NEIGHB + 1):
            here = (rows == j) & (first_half if k % 2 == 0 else ~first_half)
            index[k // 2] = jnp.where(here, others[k - 1], index[k // 2])
        weights = []
        for k in range(SLOTS):
            if k > NEIGHB:
                weights.append(jnp.zeros((BLOCK, LEVELS * BLOCK), BF16))
                continue
            if k == 0:
                weights.append(jnp.concatenate([unit] * (LEVELS // 2), axis=1))
                continue
            apart = jnp.full((BLOCK, WIDE), word ^ labels_ref[others[k - 1]], I32)
            weights.append(
                jnp.concatenate(
                    [
                        unit * jnp.where((apart & digits[t]) == 0, F32(1.0), F32(0.0)).astype(BF16)
                        for t in range(LEVELS // 2)
                    ],
                    axis=1,
                )
            )
        total = product(ops_ref[j * BLOCK : (j + 1) * BLOCK, :], jnp.concatenate(weights, axis=0))
        for level in range(LEVELS):
            lanes = slice(level // 2 * WIDE, (level // 2 + 1) * WIDE)
            mine = left if level % 2 == 0 else ~left
            acc_ref[own[level], :, lanes] = acc_ref[own[level], :, lanes] + jnp.where(mine, total[:, lanes], 0.0)
    for q in range(PAIRS):
        cols_ref[q] = index[q]
    for level in range(LEVELS):
        cols_ref[PAIRS + level] = level_cols[level]
    for t in range(LEVELS // 2):
        for q in range(PAIRS):
            even, odd = (acc_ref[2 * q + i, :, t * WIDE : (t + 1) * WIDE] for i in range(2))
            tiles_ref[2 * t, q] = jnp.where(left, even, pltpu.roll(odd, BLOCK, 1))
            tiles_ref[2 * t + 1, q] = jnp.where(left, pltpu.roll(even, BLOCK, 1), odd)


HEAD = 2 * ROWS
HALF = BLOCK // 2
SEND0 = HEAD + PAIRS * BLOCK + 2 * BLOCK
SEND1 = HEAD + 2 * BLOCK + BLOCK
SEND2 = HEAD + BLOCK + HALF
SEND3 = HEAD + HALF


def on_diagonal(size, start):
    return iota((size, WIDE), 0) + start == iota((size, WIDE), 1) % BLOCK


def packed(values, parts):
    rows = iota((ROWS, WIDE), 0)
    near = values.astype(BF16).astype(F32)
    head = jnp.where(iota((ROWS, WIDE), 1) < BLOCK, near, values - near)
    lows = jnp.zeros((ROWS, WIDE), F32)
    body = []
    for i, (part, start) in enumerate(parts):
        high, low = split(part)
        body.append(high)
        along = jnp.where(on_diagonal(part.shape[0], start), low.astype(F32), 0.0)
        lows = jnp.where(rows == i, jnp.sum(along, axis=0, keepdims=True), lows)
    return jnp.concatenate([jnp.concatenate([head, lows], axis=0).astype(BF16)] + body, axis=0)


def got_rows(ref, base):
    head = ref[base : base + HEAD, :].astype(F32)[:ROWS]
    return head + pltpu.roll(head, BLOCK, 1)


def got_part(ref, base, i, at, size, start):
    low = ref[base : base + HEAD, :].astype(F32)[ROWS + i : ROWS + i + 1]
    high = ref[base + at : base + at + size, :].astype(F32)
    return high + jnp.where(on_diagonal(size, start), low, 0.0)


def resid_kernel(ops_ref, resid_ref, rounded_ref, earlier_ref, cols_ref, tiles_ref, fresid_ref, rows_ref, send_ref):
    own = rounded_ref[...].astype(F32)
    before = earlier_ref[...].astype(F32)
    tiles = gathered(cols_ref, own)
    tiles[-1] = jnp.where(iota((ROWS, WIDE), 1) < BLOCK, tiles[-1], before)
    stacked = jnp.concatenate(tiles, axis=1)
    stacked = jnp.concatenate([stacked, jnp.zeros_like(stacked)], axis=0).astype(BF16)
    fresid = twice(resid_ref[...]) - fold(product_nt(stacked, ops_ref[...])[:ROWS])
    fresid_ref[...] = fresid
    rows = restricted(cols_ref[PAIRS], fresid)
    rows_ref[...] = rows
    other = 1 - lax.rem(lax.axis_index("gy"), 2)
    parts = [(tiles_ref[0, q], 0) for q in range(PAIRS)] + [(tiles_ref[1, 2 * other + i], 0) for i in range(2)]
    send_ref[...] = packed(rows, parts)


def descend(level, pairs, coarse_rows, ops_ref, cols_ref, fresid_ref, total_ref, fresid_out, total_out):
    out = smooth(pairs, coarse_rows)
    on_fine = picked(cols_ref[PAIRS + level], out)
    total_out[...] = total_ref[...] + on_fine
    fresid = fresid_ref[...] - ops_product(ops_ref, gathered(cols_ref, on_fine))
    if fresid_out is not None:
        fresid_out[...] = fresid
    return restricted(cols_ref[PAIRS + level + 1], fresid)


def level0_kernel(ops_ref, cols_ref, tiles_ref, rows_ref, got_ref, fresid_ref, total_ref, fresid_out, total_out, send_ref):
    half = lax.rem(lax.axis_index("gy"), 2)
    received = [got_part(got_ref, 0, i, HEAD + i * BLOCK, BLOCK, 0) for i in range(PAIRS + 2)]
    pairs = [tiles_ref[0, q] + received[q] for q in range(PAIRS)]
    coarse_rows = rows_ref[...] + got_rows(got_ref, 0)
    summed = [tiles_ref[1, 2 * half + i] + received[PAIRS + i] for i in range(2)]
    rows = descend(0, pairs, coarse_rows, ops_ref, cols_ref, fresid_ref, total_ref, fresid_out, total_out)
    for e in range(4):
        parts = [(summed[0], 0), (summed[1], 0), (tiles_ref[2, e], 0)]
        send_ref[e * SEND1 : (e + 1) * SEND1, :] = packed(rows, parts)


def level1_kernel(ops_ref, cols_ref, tiles_ref, got_ref, fresid_ref, total_ref, fresid_out, total_out, send_ref):
    coarse_rows = sum(got_rows(got_ref, e * SEND1) for e in range(4))
    pairs = []
    for q in range(PAIRS):
        half, i = q // 2, q % 2
        pairs.append(
            sum(got_part(got_ref, e * SEND1, i, HEAD + i * BLOCK, BLOCK, 0) for e in (half, half + 2))
        )
    summed = sum(got_part(got_ref, e * SEND1, 2, HEAD + 2 * BLOCK, BLOCK, 0) for e in range(4))
    rows = descend(1, pairs, coarse_rows, ops_ref, cols_ref, fresid_ref, total_ref, fresid_out, total_out)
    for e in range(8):
        start = HALF * (e % 2)
        parts = [(summed, 0), (tiles_ref[3, e // 2, start : start + HALF, :], start)]
        send_ref[e * SEND2 : (e + 1) * SEND2, :] = packed(rows, parts)


def level2_kernel(ops_ref, cols_ref, got_ref, fresid_ref, total_ref, total_out, rows_out, part_out, send_ref):
    coarse_rows = sum(got_rows(got_ref, e * SEND2) for e in range(8))
    pairs = [
        sum(got_part(got_ref, e * SEND2, 0, HEAD, BLOCK, 0) for e in (q, q + 4)) for q in range(PAIRS)
    ]
    start = HALF * lax.rem(lax.axis_index("gy"), 2)
    summed = sum(got_part(got_ref, e * SEND2, 1, HEAD + BLOCK, HALF, start) for e in range(8))
    rows = descend(2, pairs, coarse_rows, ops_ref, cols_ref, fresid_ref, total_ref, None, total_out)
    rows_out[...] = rows
    part_out[...] = summed
    send_ref[...] = packed(rows, [(summed, start)])


def join_kernel(rows_ref, part_ref, got_ref, send_ref):
    start = HALF * lax.rem(lax.axis_index("gy"), 2)
    rows = rows_ref[...] + got_rows(got_ref, 0)
    chunk = packed(rows, [(part_ref[...] + got_part(got_ref, 0, 0, HEAD, HALF, start), start)])
    for e in range(8):
        send_ref[e * SEND3 : (e + 1) * SEND3, :] = chunk


def level3_kernel(cols_ref, got_ref, total_ref, out_ref):
    coarse_rows = sum(got_rows(got_ref, e * SEND3) for e in range(8))
    eighths = [got_part(got_ref, e * SEND3, 0, HEAD, HALF, HALF * (e % 2)) for e in range(8)]
    pairs = [jnp.concatenate([eighths[2 * q], eighths[2 * q + 1]], axis=0) for q in range(PAIRS)]
    out = smooth(pairs, coarse_rows)
    out_ref[...] = (total_ref[...] + picked(cols_ref[PAIRS + 3], out))[:, :BLOCK]


def call(kernel, name, out_shapes, args, scalars=0, scratch=(), outside=0):
    hbm = pl.BlockSpec(memory_space=pltpu.HBM)
    vmem = pl.BlockSpec(memory_space=pltpu.VMEM)
    smem = pl.BlockSpec(memory_space=pltpu.SMEM)
    return pl.pallas_call(
        kernel,
        name=name,
        out_shape=[jax.ShapeDtypeStruct(shape, kind) for shape, kind in out_shapes],
        in_specs=[smem] * scalars + [hbm] * outside + [vmem] * (len(args) - scalars - outside),
        out_specs=[vmem] * len(out_shapes),
        scratch_shapes=list(scratch),
        compiler_params=pltpu.CompilerParams(vmem_limit_bytes=GRANT),
        interpret=INTERPRET,
    )(*args)


def shared(chunks, size):
    lists = [[g * size + i for i in range(size)] for g in range(lax.axis_size("gy") // size)]
    return lax.all_to_all(chunks, "gy", 0, 0, axis_index_groups=lists, tiled=True)


def crossed(value, distance):
    return lax.ppermute(value, "gy", [(i, i ^ distance) for i in range(lax.axis_size("gy"))])


def on_device(residual, fine_ops, neighbours, fine_map, coarse_maps):
    ops = fine_ops.reshape(FINE_BLOCKS * BLOCK, SLOTS * BLOCK)
    vec = (FINE_BLOCKS, WIDE)
    fine_smooth, rounded = call(
        fine_kernel,
        "fine_smooth",
        [(vec, F32), (vec, BF16)],
        [pltpu.with_memory_space_constraint(x, pltpu.HBM) for x in (ops, residual)],
        outside=2,
        scratch=[
            pltpu.VMEM((FINE_BLOCKS * BLOCK, WIDE), BF16),
            pltpu.VMEM((FINE_BLOCKS, BLOCK), F32),
            pltpu.SemaphoreType.DMA,
            pltpu.SemaphoreType.DMA,
        ],
    )
    earlier = lax.ppermute(rounded, "ta", [(0, 1)])
    cols, tiles = call(
        tiles_kernel,
        "tile_parts",
        [((PAIRS + LEVELS, ROWS, WIDE), I32), ((LEVELS, PAIRS, BLOCK, WIDE), F32)],
        [neighbours, fine_map, jnp.transpose(coarse_maps, (1, 0, 2)), ops],
        scalars=3,
        scratch=[pltpu.VMEM((COARSE, BLOCK, LEVELS * BLOCK), F32), pltpu.SMEM((FINE_BLOCKS,), I32)],
    )
    fresid, rows, sent = call(
        resid_kernel,
        "fine_resid",
        [(vec, F32), (vec, F32), ((SEND0, WIDE), BF16)],
        [ops, residual, rounded, earlier, cols, tiles],
    )
    got = crossed(sent, 1)
    fresid, total, chunks = call(
        level0_kernel,
        "level_0",
        [(vec, F32), (vec, F32), ((4 * SEND1, WIDE), BF16)],
        [ops, cols, tiles, rows, got, fresid, fine_smooth],
    )
    got = shared(chunks, 4)
    fresid, total, chunks = call(
        level1_kernel,
        "level_1",
        [(vec, F32), (vec, F32), ((8 * SEND2, WIDE), BF16)],
        [ops, cols, tiles, got, fresid, total],
    )
    got = shared(chunks, 8)
    total, rows, part, sent = call(
        level2_kernel,
        "level_2",
        [(vec, F32), (vec, F32), ((HALF, WIDE), F32), ((SEND3, WIDE), BF16)],
        [ops, cols, got, fresid, total],
    )
    got = crossed(sent, 8)
    (chunks,) = call(join_kernel, "join", [((8 * SEND3, WIDE), BF16)], [rows, part, got])
    got = shared(chunks, 8)
    (out,) = call(level3_kernel, "level_3", [((FINE_BLOCKS, BLOCK), F32)], [cols, got, total])
    return out


def solution(mesh):
    return jax.shard_map(
        on_device,
        mesh=mesh,
        in_specs=(
            P(("gx", "gy", "ta"), None),
            P(("gx", "gy", "ta"), None, None),
            P(("gx", "gy", "ta"), None),
            P(("gx", "gy", "ta")),
            P(("gx", "gy", "ta"), None, None),
        ),
        out_specs=P(("gx", "gy", "ta"), None),
        check_vma=False,
    )
```

```python
import jax
import jax.numpy as jnp
from jax import lax
from jax.experimental import pallas as pl
from jax.experimental.pallas import tpu as pltpu
from jax.sharding import PartitionSpec as P

BLOCK = 64
SLOTS = 8
NEIGHB = 6
COARSE = 8
LEVELS = 4
FINE_BLOCKS = 8
PAIRS = COARSE // 2
WIDE = 2 * BLOCK
ROWS = COARSE
GRANT = 12 * 2**20
INTERPRET = False

F32 = jnp.float32
BF16 = jnp.bfloat16
I32 = jnp.int32


def iota(shape, axis):
    return lax.broadcasted_iota(I32, shape, axis)


def product(x, weights):
    return jnp.dot(x, weights, preferred_element_type=F32)


def product_nt(x, weights):
    return lax.dot_general(x, weights, (((1,), (1,)), ((), ())), preferred_element_type=F32)


def split(x):
    high = x.astype(BF16)
    return high, (x - high.astype(F32)).astype(BF16)


def split_rows(x):
    high = x.astype(BF16).astype(F32)
    return jnp.concatenate([high, x - high], axis=0).astype(BF16)


def twice(x):
    return jnp.concatenate([x, x], axis=1)


def own_lanes(pair):
    return iota((ROWS, WIDE), 0) == 2 * pair + iota((ROWS, WIDE), 1) // BLOCK


def spread(values):
    return jnp.concatenate([jnp.where(own_lanes(q), values, 0.0) for q in range(PAIRS)], axis=1)


def fold(wide):
    kept = sum(jnp.where(own_lanes(q), wide[:, q * WIDE : (q + 1) * WIDE], 0.0) for q in range(PAIRS))
    return kept + pltpu.roll(kept, BLOCK, 1)


def squared(error):
    left = (iota((BLOCK, WIDE), 1) < BLOCK).astype(F32).astype(BF16)
    right = (iota((BLOCK, WIDE), 1) >= BLOCK).astype(F32).astype(BF16)
    high, low = split(error)
    weights = jnp.concatenate(
        [
            jnp.concatenate([high * left, high * right], axis=0),
            jnp.concatenate([low * left, low * right], axis=0),
        ],
        axis=1,
    )
    full = product(jnp.concatenate([high, low], axis=0), weights)
    top = full[:BLOCK] + full[BLOCK:]
    return top[:, :WIDE] + top[:, WIDE:]


def operand(errors):
    parts = [split(one) for one in errors]
    return jnp.concatenate(
        [jnp.concatenate([h for h, _ in parts], axis=1), jnp.concatenate([l for _, l in parts], axis=1)],
        axis=0,
    )


def applied(weights, values):
    full = product_nt(split_rows(spread(values)), weights)
    top = full[:ROWS] + full[ROWS:]
    return top + pltpu.roll(top, BLOCK, 1)


def smooth(pairs, values):
    eye = iota((BLOCK, WIDE), 0) == iota((BLOCK, WIDE), 1) % BLOCK
    sums = sum(
        jnp.where(own_lanes(q), jnp.sum(jnp.where(eye, pairs[q], 0.0), axis=0, keepdims=True), 0.0)
        for q in range(PAIRS)
    )
    inverse = 1.0 / (jnp.sum(sums, axis=1, keepdims=True) * (1.0 / BLOCK))
    one = eye.astype(F32)
    first = []
    for q in range(PAIRS):
        along = jnp.sum(jnp.where(own_lanes(q), inverse, 0.0), axis=0, keepdims=True)
        first.append(one - pairs[q] * along)
    y = values + applied(operand(first), values)
    second = [squared(e) for e in first]
    y = y + applied(operand(second), y)
    fourth = [squared(e) for e in second]
    y = y + applied(operand(fourth), y)
    y = y + applied(operand([squared(e) for e in fourth]), y)
    return y * inverse


def picked(index, values):
    return sum(jnp.where(index == x, values[x : x + 1], 0.0) for x in range(COARSE))


def restricted(index, values):
    total = jnp.zeros_like(values)
    for x in range(COARSE):
        row = jnp.sum(jnp.where(index == x, values, 0.0), axis=0, keepdims=True)
        total = total + jnp.where(iota(values.shape, 0) == x, row, 0.0)
    return total


def gathered(maps_ref, doubled):
    return [picked(maps_ref[q], doubled) for q in range(PAIRS)]


def ops_product(ops_ref, tiles):
    stacked = split_rows(jnp.concatenate(tiles, axis=1))
    full = product_nt(stacked, ops_ref[...])
    return fold(full[:ROWS] + full[ROWS:])


def fine_kernel(ops_hbm, resid_hbm, smooth_ref, rounded_ref, zeros_ref, diag_ref, resid_ref, diag_sem, resid_sem):
    diag_copy = pltpu.make_async_copy(ops_hbm.at[:, :WIDE], diag_ref, diag_sem)
    resid_copy = pltpu.make_async_copy(resid_hbm, resid_ref, resid_sem)
    diag_copy.start()
    resid_copy.start()
    zeros_ref[...] = jnp.zeros_like(zeros_ref)
    diag_copy.wait()
    resid_copy.wait()
    pairs = []
    for q in range(PAIRS):
        even = diag_ref[2 * q * BLOCK : (2 * q + 1) * BLOCK, :BLOCK].astype(F32)
        odd = diag_ref[(2 * q + 1) * BLOCK : (2 * q + 2) * BLOCK, :BLOCK].astype(F32)
        pairs.append(jnp.concatenate([even, odd], axis=1))
    out = smooth(pairs, twice(resid_ref[...]))
    smooth_ref[...] = out
    rounded_ref[...] = out.astype(BF16)


def tiles_kernel(near_ref, fine_map_ref, maps_ref, ops_ref, zeros_ref, cols_ref, tiles_ref, acc_ref, labels_ref):
    left = iota((BLOCK, WIDE), 1) < BLOCK
    unit = (iota((BLOCK, WIDE), 0) == iota((BLOCK, WIDE), 1) % BLOCK).astype(F32).astype(BF16)
    digits = [jnp.where(left, 7 * 8 ** (2 * t), 7 * 8 ** (2 * t + 1)) for t in range(LEVELS // 2)]
    rows = iota((ROWS, WIDE), 0)
    first_half = iota((ROWS, WIDE), 1) < BLOCK

    owns = []
    for j in range(FINE_BLOCKS):
        own = [fine_map_ref[j]]
        for level in range(LEVELS - 1):
            own.append(maps_ref[level, 0, own[-1]])
        word = own[0]
        for level in range(1, LEVELS):
            word = word + own[level] * 8**level
        labels_ref[j] = word
        owns.append((own, word))

    index = [jnp.where(first_half, rows, -1)] + [jnp.full((ROWS, WIDE), -1, I32) for q in range(PAIRS - 1)]
    level_cols = [jnp.zeros((ROWS, WIDE), I32) for level in range(LEVELS)]
    for j in range(FINE_BLOCKS):
        own, word = owns[j]
        others = [near_ref[j, k] for k in range(NEIGHB)]
        for level in range(LEVELS):
            level_cols[level] = jnp.where(rows == j, own[level], level_cols[level])
        for k in range(1, NEIGHB + 1):
            here = (rows == j) & (first_half if k % 2 == 0 else ~first_half)
            index[k // 2] = jnp.where(here, others[k - 1], index[k // 2])
        weights = []
        for k in range(SLOTS):
            if k > NEIGHB:
                weights.append(jnp.zeros((BLOCK, LEVELS * BLOCK), BF16))
                continue
            if k == 0:
                weights.append(jnp.concatenate([unit] * (LEVELS // 2), axis=1))
                continue
            apart = jnp.full((BLOCK, WIDE), word ^ labels_ref[others[k - 1]], I32)
            weights.append(
                jnp.concatenate(
                    [
                        unit * jnp.where((apart & digits[t]) == 0, F32(1.0), F32(0.0)).astype(BF16)
                        for t in range(LEVELS // 2)
                    ],
                    axis=1,
                )
            )
        total = product(ops_ref[j * BLOCK : (j + 1) * BLOCK, :], jnp.concatenate(weights, axis=0))
        for level in range(LEVELS):
            lanes = slice(level // 2 * WIDE, (level // 2 + 1) * WIDE)
            mine = left if level % 2 == 0 else ~left
            acc_ref[own[level], :, lanes] = acc_ref[own[level], :, lanes] + jnp.where(mine, total[:, lanes], 0.0)
    for q in range(PAIRS):
        cols_ref[q] = index[q]
    for level in range(LEVELS):
        cols_ref[PAIRS + level] = level_cols[level]
    for t in range(LEVELS // 2):
        for q in range(PAIRS):
            even, odd = (acc_ref[2 * q + i, :, t * WIDE : (t + 1) * WIDE] for i in range(2))
            tiles_ref[2 * t, q] = jnp.where(left, even, pltpu.roll(odd, BLOCK, 1))
            tiles_ref[2 * t + 1, q] = jnp.where(left, pltpu.roll(even, BLOCK, 1), odd)


HEAD = 2 * ROWS
HALF = BLOCK // 2
SEND0 = HEAD + PAIRS * BLOCK + 2 * BLOCK
SEND1 = HEAD + 2 * BLOCK + BLOCK
SEND2 = HEAD + BLOCK + HALF
SEND3 = HEAD + HALF


def on_diagonal(size, start):
    return iota((size, WIDE), 0) + start == iota((size, WIDE), 1) % BLOCK


def packed(values, parts):
    rows = iota((ROWS, WIDE), 0)
    near = values.astype(BF16).astype(F32)
    head = jnp.where(iota((ROWS, WIDE), 1) < BLOCK, near, values - near)
    lows = jnp.zeros((ROWS, WIDE), F32)
    body = []
    for i, (part, start) in enumerate(parts):
        high, low = split(part)
        body.append(high)
        along = jnp.where(on_diagonal(part.shape[0], start), low.astype(F32), 0.0)
        lows = jnp.where(rows == i, jnp.sum(along, axis=0, keepdims=True), lows)
    return jnp.concatenate([jnp.concatenate([head, lows], axis=0).astype(BF16)] + body, axis=0)


def got_rows(ref, base):
    head = ref[base : base + HEAD, :].astype(F32)[:ROWS]
    return head + pltpu.roll(head, BLOCK, 1)


def got_part(ref, base, i, at, size, start):
    low = ref[base : base + HEAD, :].astype(F32)[ROWS + i : ROWS + i + 1]
    high = ref[base + at : base + at + size, :].astype(F32)
    return high + jnp.where(on_diagonal(size, start), low, 0.0)


def resid_kernel(ops_ref, resid_ref, rounded_ref, earlier_ref, cols_ref, tiles_ref, fresid_ref, rows_ref, send_ref):
    own = rounded_ref[...].astype(F32)
    before = earlier_ref[...].astype(F32)
    tiles = gathered(cols_ref, own)
    tiles[-1] = jnp.where(iota((ROWS, WIDE), 1) < BLOCK, tiles[-1], before)
    stacked = jnp.concatenate(tiles, axis=1)
    stacked = jnp.concatenate([stacked, jnp.zeros_like(stacked)], axis=0).astype(BF16)
    fresid = twice(resid_ref[...]) - fold(product_nt(stacked, ops_ref[...])[:ROWS])
    fresid_ref[...] = fresid
    rows = restricted(cols_ref[PAIRS], fresid)
    rows_ref[...] = rows
    other = 1 - lax.rem(lax.axis_index("gy"), 2)
    parts = [(tiles_ref[0, q], 0) for q in range(PAIRS)] + [(tiles_ref[1, 2 * other + i], 0) for i in range(2)]
    send_ref[...] = packed(rows, parts)


def descend(level, pairs, coarse_rows, ops_ref, cols_ref, fresid_ref, total_ref, fresid_out, total_out):
    out = smooth(pairs, coarse_rows)
    on_fine = picked(cols_ref[PAIRS + level], out)
    total_out[...] = total_ref[...] + on_fine
    fresid = fresid_ref[...] - ops_product(ops_ref, gathered(cols_ref, on_fine))
    if fresid_out is not None:
        fresid_out[...] = fresid
    return restricted(cols_ref[PAIRS + level + 1], fresid)


def level0_kernel(ops_ref, cols_ref, tiles_ref, rows_ref, got_ref, fresid_ref, total_ref, fresid_out, total_out, send_ref):
    half = lax.rem(lax.axis_index("gy"), 2)
    received = [got_part(got_ref, 0, i, HEAD + i * BLOCK, BLOCK, 0) for i in range(PAIRS + 2)]
    pairs = [tiles_ref[0, q] + received[q] for q in range(PAIRS)]
    coarse_rows = rows_ref[...] + got_rows(got_ref, 0)
    summed = [tiles_ref[1, 2 * half + i] + received[PAIRS + i] for i in range(2)]
    rows = descend(0, pairs, coarse_rows, ops_ref, cols_ref, fresid_ref, total_ref, fresid_out, total_out)
    for e in range(4):
        parts = [(summed[0], 0), (summed[1], 0), (tiles_ref[2, e], 0)]
        send_ref[e * SEND1 : (e + 1) * SEND1, :] = packed(rows, parts)


def level1_kernel(ops_ref, cols_ref, tiles_ref, got_ref, fresid_ref, total_ref, fresid_out, total_out, send_ref):
    coarse_rows = sum(got_rows(got_ref, e * SEND1) for e in range(4))
    pairs = []
    for q in range(PAIRS):
        half, i = q // 2, q % 2
        pairs.append(
            sum(got_part(got_ref, e * SEND1, i, HEAD + i * BLOCK, BLOCK, 0) for e in (half, half + 2))
        )
    summed = sum(got_part(got_ref, e * SEND1, 2, HEAD + 2 * BLOCK, BLOCK, 0) for e in range(4))
    rows = descend(1, pairs, coarse_rows, ops_ref, cols_ref, fresid_ref, total_ref, fresid_out, total_out)
    for e in range(8):
        start = HALF * (e % 2)
        parts = [(summed, 0), (tiles_ref[3, e // 2, start : start + HALF, :], start)]
        send_ref[e * SEND2 : (e + 1) * SEND2, :] = packed(rows, parts)


def level2_kernel(ops_ref, cols_ref, got_ref, fresid_ref, total_ref, total_out, rows_out, part_out, send_ref):
    coarse_rows = sum(got_rows(got_ref, e * SEND2) for e in range(8))
    pairs = [
        sum(got_part(got_ref, e * SEND2, 0, HEAD, BLOCK, 0) for e in (q, q + 4)) for q in range(PAIRS)
    ]
    start = HALF * lax.rem(lax.axis_index("gy"), 2)
    summed = sum(got_part(got_ref, e * SEND2, 1, HEAD + BLOCK, HALF, start) for e in range(8))
    rows = descend(2, pairs, coarse_rows, ops_ref, cols_ref, fresid_ref, total_ref, None, total_out)
    rows_out[...] = rows
    part_out[...] = summed
    send_ref[...] = packed(rows, [(summed, start)])


def join_kernel(rows_ref, part_ref, got_ref, send_ref):
    start = HALF * lax.rem(lax.axis_index("gy"), 2)
    rows = rows_ref[...] + got_rows(got_ref, 0)
    chunk = packed(rows, [(part_ref[...] + got_part(got_ref, 0, 0, HEAD, HALF, start), start)])
    for e in range(8):
        send_ref[e * SEND3 : (e + 1) * SEND3, :] = chunk


def level3_kernel(cols_ref, got_ref, total_ref, out_ref):
    coarse_rows = sum(got_rows(got_ref, e * SEND3) for e in range(8))
    eighths = [got_part(got_ref, e * SEND3, 0, HEAD, HALF, HALF * (e % 2)) for e in range(8)]
    pairs = [jnp.concatenate([eighths[2 * q], eighths[2 * q + 1]], axis=0) for q in range(PAIRS)]
    out = smooth(pairs, coarse_rows)
    out_ref[...] = (total_ref[...] + picked(cols_ref[PAIRS + 3], out))[:, :BLOCK]


def call(kernel, name, out_shapes, args, scalars=0, scratch=(), outside=0, aliases={}):
    hbm = pl.BlockSpec(memory_space=pltpu.HBM)
    vmem = pl.BlockSpec(memory_space=pltpu.VMEM)
    smem = pl.BlockSpec(memory_space=pltpu.SMEM)
    return pl.pallas_call(
        kernel,
        name=name,
        out_shape=[jax.ShapeDtypeStruct(shape, kind) for shape, kind in out_shapes],
        in_specs=[smem] * scalars + [hbm] * outside + [vmem] * (len(args) - scalars - outside),
        out_specs=[vmem] * len(out_shapes),
        scratch_shapes=list(scratch),
        compiler_params=pltpu.CompilerParams(vmem_limit_bytes=GRANT),
        input_output_aliases=aliases,
        interpret=INTERPRET,
    )(*args)


def shared(chunks, size):
    lists = [[g * size + i for i in range(size)] for g in range(lax.axis_size("gy") // size)]
    return lax.all_to_all(chunks, "gy", 0, 0, axis_index_groups=lists, tiled=True)


def crossed(value, distance):
    return lax.ppermute(value, "gy", [(i, i ^ distance) for i in range(lax.axis_size("gy"))])


def on_device(residual, fine_ops, neighbours, fine_map, coarse_maps):
    ops = fine_ops.reshape(FINE_BLOCKS * BLOCK, SLOTS * BLOCK)
    vec = (FINE_BLOCKS, WIDE)
    share = ((COARSE, BLOCK, LEVELS * BLOCK), F32)
    fine_smooth, rounded, zeros = call(
        fine_kernel,
        "fine_smooth",
        [(vec, F32), (vec, BF16), share],
        [pltpu.with_memory_space_constraint(x, pltpu.HBM) for x in (ops, residual)],
        outside=2,
        scratch=[
            pltpu.VMEM((FINE_BLOCKS * BLOCK, WIDE), BF16),
            pltpu.VMEM((FINE_BLOCKS, BLOCK), F32),
            pltpu.SemaphoreType.DMA,
            pltpu.SemaphoreType.DMA,
        ],
    )
    earlier = lax.ppermute(rounded, "ta", [(0, 1)])
    cols, tiles, _ = call(
        tiles_kernel,
        "tile_parts",
        [((PAIRS + LEVELS, ROWS, WIDE), I32), ((LEVELS, PAIRS, BLOCK, WIDE), F32), share],
        [neighbours, fine_map, jnp.transpose(coarse_maps, (1, 0, 2)), ops, zeros],
        scalars=3,
        scratch=[pltpu.SMEM((FINE_BLOCKS,), I32)],
        aliases={4: 2},
    )
    fresid, rows, sent = call(
        resid_kernel,
        "fine_resid",
        [(vec, F32), (vec, F32), ((SEND0, WIDE), BF16)],
        [ops, residual, rounded, earlier, cols, tiles],
    )
    got = crossed(sent, 1)
    fresid, total, chunks = call(
        level0_kernel,
        "level_0",
        [(vec, F32), (vec, F32), ((4 * SEND1, WIDE), BF16)],
        [ops, cols, tiles, rows, got, fresid, fine_smooth],
    )
    got = shared(chunks, 4)
    fresid, total, chunks = call(
        level1_kernel,
        "level_1",
        [(vec, F32), (vec, F32), ((8 * SEND2, WIDE), BF16)],
        [ops, cols, tiles, got, fresid, total],
    )
    got = shared(chunks, 8)
    total, rows, part, sent = call(
        level2_kernel,
        "level_2",
        [(vec, F32), (vec, F32), ((HALF, WIDE), F32), ((SEND3, WIDE), BF16)],
        [ops, cols, got, fresid, total],
    )
    got = crossed(sent, 8)
    (chunks,) = call(join_kernel, "join", [((8 * SEND3, WIDE), BF16)], [rows, part, got])
    got = shared(chunks, 8)
    (out,) = call(level3_kernel, "level_3", [((FINE_BLOCKS, BLOCK), F32)], [cols, got, total])
    return out


def solution(mesh):
    return jax.shard_map(
        on_device,
        mesh=mesh,
        in_specs=(
            P(("gx", "gy", "ta"), None),
            P(("gx", "gy", "ta"), None, None),
            P(("gx", "gy", "ta"), None),
            P(("gx", "gy", "ta")),
            P(("gx", "gy", "ta"), None, None),
        ),
        out_specs=P(("gx", "gy", "ta"), None),
        check_vma=False,
    )
```
